128 devices in a mesh: req: 8 (over z, core), exp: 16 (over y, x).
Axes of the slice: x: 4, y: 4, z: 4, core: 2. Of those that a mesh axis runs over, the one named last changes fastest.
Arguments:
- hidden_in: bfloat16 [16, 16, 64, 2048], P('exp', 'req'), may hold values from -6 to 6
- router_choice: int32 [16, 16, 64, 2], P('exp', 'req'), may hold values from 0 to 7, all different within a row; in each aligned block of 128 rows (0 to 127, 128 to 255, ..., all dimensions but the last counted through in order) at most 48 rows name the same one
- w_router: bfloat16 [2048, 8], replicated, may hold values from -0.125 to 0.125
- w_kv: bfloat16 [2048, 2048], replicated, may hold values from -0.125 to 0.125
- w_query: bfloat16 [16, 2048, 512], P('exp'), may hold values from -0.125 to 0.125
- w_out: bfloat16 [16, 512, 2048], P('exp'), may hold values from -0.75 to 0.75
- kv_cache: bfloat16 [16, 128, 128, 2048], P('exp', 'req'), may hold values from -68 to 68
- page_count: int32 [16, 16], P('exp'), may hold values from 1 to 32, 128 in all within a row
- tail_len: int32 [16, 16], P('exp'), may hold values from 1 to 128
- page_perm: int32 [16, 128], P('exp'), may hold values from 0 to 127, each once within a row
- parents: int32 [16, 16, 64], P('exp', 'req'), may hold values from 0 to 62, as said below
- accepted_leaf: int32 [16, 16], P('exp', 'req'), may hold values from 0 to 63
Outputs:
- attn_out: bfloat16 [16, 16, 64, 2048], P('exp', 'req')
- cache_rows: bfloat16 [16, 16, 64, 2048], P('exp', 'req')
The draws below stay inside these ranges and needn't reach their ends.
Inputs may be any that keep to these rules, and one draw needn't show every extreme that they name: `router_choice`: in the rows of one device (aligned blocks of 128 rows), no expert is named by more than 48 rows, and 48 is reached. `page_count`: each row sums to 128; its largest entry is 32. `page_perm`: each row holds each number once. parents of token 0 is 0; for j >= 1 parents of token j is below j; the last token's parent is token 62.
All inputs are finite; a program needn't handle non-finite values.
Results may differ from the reference program's by a relative error of at most 0.014.
The reference program's roundings to bfloat16 on the way count: a program that leaves them out, or rounds other values in their place, can miss the bound.
Values may be sent and summed in bfloat16 or wider, within the bound.
A program may use at most 128 MiB of HBM per device.

```python
import math
import jax
import jax.numpy as jnp
import numpy as np
from jax import lax

D = 2048
HD = 128
EXPERTS = 8
KVH = 8
TOPK = 2
PAGE = 128
DRAFT = 64
REQ_X = 2
SLOTS = 16
HEADS_DEV = 4
GREQ = 16
POOL = 128
CAP = 48
MAXP = 32
N_REQ = 8
N_EXP = 16


def draw_kv_cache(key, part):
    full_shape = (N_EXP, N_REQ * SLOTS, PAGE, 2 * KVH * HD)
    values_all = jax.random.truncated_normal(key, -6.0, 6.0, full_shape, jnp.float32)
    return values_all.astype(jnp.bfloat16)


def draw_parents(key, part):
    token_index = jnp.arange(DRAFT, dtype=jnp.int32)
    upper_bound = jnp.maximum(token_index, 1)
    drawn = jax.random.randint(key, (N_EXP, N_REQ * REQ_X, DRAFT), 0, upper_bound, dtype=jnp.int32)
    drawn = jnp.where(token_index == DRAFT - 1, DRAFT - 2, drawn)
    return jnp.where(token_index == 0, 0, drawn).astype(jnp.int32)


def place_ends(array, own_key, low, largest):
    index_at = [jax.random.randint(jax.random.fold_in(own_key, axis), (), 0, length) for axis, length in enumerate(array.shape)]
    main_axis = array.shape.index(max(array.shape))
    next_to = index_at[:main_axis] + [(index_at[main_axis] + 1) % array.shape[main_axis]] + index_at[main_axis + 1:]
    return array.at[tuple(index_at)].set(low).at[tuple(next_to)].set(largest)


def block_levels(rng, extent, shards, low, top_value):
    level, own = 1.0, jax.random.fold_in(rng, 6)
    for axis_at, blocks in shards:
        steps = jnp.exp(jax.random.uniform(jax.random.fold_in(own, axis_at), (blocks,), jnp.float32, low / len(shards), top_value / len(shards)))
        level = level * jnp.repeat(steps, extent[axis_at] // blocks).reshape([-1 if axis == axis_at else 1 for axis in range(len(extent))])
    return level


def length_profile(amount, total, bound, slope):
    portions = [(1 << 20) // math.isqrt(grade ** slope) + 1 for grade in range(2, amount + 1)]
    surplus, given = total - bound - (amount - 1), [1] * (amount - 1)
    while surplus > 0:
        candidates = [i for i in range(amount - 1) if given[i] < bound]
        whole, remaining = sum([portions[i] for i in candidates]), surplus
        for i in candidates:
            extra = min(bound - given[i], max(1, remaining * portions[i] // whole), surplus)
            given[i] = given[i] + extra
            surplus = surplus - extra
    return np.array([bound] + given)


def ragged_sizes(key, count, total, bound, lean):
    if count == 2:
        one = jax.random.randint(key, (), max(1, total - bound), min(bound, total - 1) + 1)
        return jnp.stack([one, total - one])
    sizes = jnp.asarray(length_profile(count, total, bound, lean), jnp.int32)
    twos = (count - 1) // 2
    donor, taker = sizes[1:1 + 2 * twos:2], sizes[2:2 + 2 * twos:2]
    margin = jnp.minimum(donor - 1, bound - taker)
    passed = jax.random.randint(jax.random.fold_in(key, 1), (twos,), 0, 1 << 20) % (margin + 1)
    sizes = sizes.at[1:1 + 2 * twos:2].set(donor - passed).at[2:2 + 2 * twos:2].set(taker + passed)
    return sizes[jax.random.permutation(jax.random.fold_in(key, 2), count)]


def assign_block(own_key, own, number, rows, number_of, top, limit, slope):
    sequence = jax.random.permutation(own_key, number_of)
    crowded, ordinary = portions_of(number_of, rows * top, limit, slope, True), portions_of(number_of, rows * top, limit, slope, False)
    places = jnp.arange(number_of)

    def named(sizes, rotation):
        used = int((sizes > 0).sum())
        fixed = max(1, used // 4)
        passed = fixed + (places - fixed + rotation * (used - fixed)) % max(1, number_of - fixed)
        return jnp.zeros((number_of,), jnp.int32).at[sequence[jnp.where(places < fixed, places, passed)]].set(jnp.asarray(sizes, jnp.int32))

    sizes = jnp.where(number % 4 == 0, named(crowded, number // 4), named(ordinary, number - number // 4 - 1))
    mixed = jax.random.permutation(jax.random.fold_in(own, 3), number_of)
    donor, sink = mixed[0:number_of // 2 * 2:2], mixed[1:number_of // 2 * 2:2]
    margin = jnp.minimum(sizes[donor] - 1, limit - sizes[sink]) // 2
    margin = jnp.where((donor == sequence[0]) | (sink == sequence[0]) | (sizes[sink] == 0), 0, jnp.maximum(margin, 0))
    passed = jax.random.randint(jax.random.fold_in(own, 4), (number_of // 2,), 0, 1 << 20) % (margin + 1)
    sizes = sizes.at[donor].add(-passed).at[sink].add(passed)
    labels = jnp.searchsorted(jnp.cumsum(sizes), jnp.arange(rows * top), side="right").astype(jnp.int32)
    grid = labels.reshape(top, rows).T
    grid = grid[jax.random.permutation(jax.random.fold_in(own, 1), rows)]
    rotation = jax.random.randint(jax.random.fold_in(own, 2), (rows, 1), 0, top)
    return jnp.take_along_axis(grid, (jnp.arange(top)[None, :] + rotation) % top, axis=1)


def portions_of(count, total, most, skew, full):
    portions = [(1 << 20) // math.isqrt(standing ** skew) + 1 for standing in range(1, count + 1)]
    largest = most if full else min(most, max(-(-total // count), total * portions[0] // sum(portions)))
    least = 1 if total - largest >= count - 1 else 0
    holding, surplus = [largest] + [least] * (count - 1), total - largest - least * (count - 1)
    while surplus > 0:
        movable = [i for i in range(1, count) if holding[i] < largest] or [i for i in range(1, count) if holding[i] < most]
        whole, left = sum([portions[i] for i in movable]), surplus
        for i in movable:
            more = min(most - holding[i], max(1, left * portions[i] // whole), surplus)
            holding[i] = holding[i] + more
            surplus = surplus - more
    return np.array(holding)


def centred(stream_key, dims, width, limit, split=(), kind=jnp.bfloat16):
    values = width * jax.random.normal(stream_key, dims, jnp.float32)
    if split:
        values = values * block_levels(stream_key, dims, split, -0.22, 0.18)
    return jnp.clip(values, -limit, limit).astype(kind)


def setup_inputs(seed: int = 0) -> dict:
    keys = jax.random.split(jax.random.key(seed), 13)
    hidden_in = centred(keys[0], (N_EXP, GREQ, DRAFT, D), 1.0, 6.0, ((0, 16), (1, 8)))
    router_choice_keys = jax.random.split(jax.random.fold_in(keys[1], 1), N_EXP * GREQ * DRAFT // (REQ_X * DRAFT))
    router_choice_turns = jax.random.permutation(jax.random.fold_in(keys[1], 3), N_EXP * GREQ * DRAFT // (REQ_X * DRAFT))
    router_choice = jax.vmap(lambda own, number: assign_block(jax.random.fold_in(keys[1], 2), own, number, REQ_X * DRAFT, EXPERTS, TOPK, CAP, 2))(router_choice_keys, router_choice_turns).reshape((N_EXP, GREQ, DRAFT, TOPK))
    w_router = centred(keys[2], (D, EXPERTS), D ** -0.5, 0.125)
    w_kv = centred(keys[3], (D, 2 * KVH * HD), D ** -0.5, 0.125)
    w_query = centred(keys[4], (N_EXP, D, HEADS_DEV * HD), D ** -0.5, 0.125, ((0, 16),))
    w_out = centred(keys[5], (N_EXP, HEADS_DEV * HD, D), 0.125, 0.75, ((0, 16),))
    kv_cache = draw_kv_cache(jax.random.fold_in(keys[12], 71), 0)
    page_count = jax.vmap(lambda own: ragged_sizes(own, GREQ, N_REQ * SLOTS, MAXP, 2))(jax.random.split(keys[7], N_EXP)).reshape((N_EXP, GREQ)).astype(jnp.int32)
    tail_len = place_ends(jax.random.randint(keys[8], (N_EXP, GREQ), 1, PAGE + 1), jax.random.fold_in(keys[8], 1), 1, PAGE).astype(jnp.int32)
    page_perm = jax.vmap(lambda own: jax.random.permutation(own, POOL))(jax.random.split(keys[9], N_EXP)).reshape((N_EXP, POOL)).astype(jnp.int32)
    parents = draw_parents(jax.random.fold_in(keys[12], 71), 0)
    accepted_leaf = place_ends(jax.random.randint(keys[11], (N_EXP, GREQ), 0, DRAFT), jax.random.fold_in(keys[11], 1), 0, DRAFT - 1).astype(jnp.int32)
    return dict(hidden_in=hidden_in, router_choice=router_choice, w_router=w_router, w_kv=w_kv, w_query=w_query, w_out=w_out, kv_cache=kv_cache, page_count=page_count, tail_len=tail_len, page_perm=page_perm, parents=parents, accepted_leaf=accepted_leaf)


NEGATIVE_FILL = -1e+30
NORM_EPSILON = 1e-06

def rotate(values_in, positions):
    half_width = values_in.shape[-1] // 2
    inverse_freq = 10000.0 ** (-jnp.arange(half_width, dtype=jnp.float32) / half_width)
    angles = positions.astype(jnp.float32)[..., None, None] * inverse_freq
    cosine_part = jnp.cos(angles)
    sine_part = jnp.sin(angles)
    leading = values_in[..., :half_width]
    trailing = values_in[..., half_width:]
    return jnp.concatenate([leading * cosine_part - trailing * sine_part, trailing * cosine_part + leading * sine_part], axis=-1)

def ancestry(parent_ids):
    count_tokens = parent_ids.shape[-1]
    index_row = jnp.arange(count_tokens, dtype=jnp.int32)
    linked = (parent_ids[..., :, None] == index_row) & (index_row[:, None] > 0)
    reachable = linked.astype(jnp.float32) + jnp.eye(count_tokens, dtype=jnp.float32)
    for doubling in range(count_tokens.bit_length()):
        reachable = jnp.minimum(jnp.matmul(reachable, reachable, precision=lax.Precision.HIGHEST), 1.0)
    return reachable

def block_partial(scores, valid, values):
    masked = jnp.where(valid, scores, NEGATIVE_FILL)
    block_max = lax.optimization_barrier(jnp.max(masked, axis=-1))
    weights = jnp.where(valid, jnp.exp(masked - block_max[..., None]), 0.0)
    block_sum = lax.optimization_barrier(jnp.sum(weights, axis=-1))
    rounded = lax.optimization_barrier(weights.astype(jnp.bfloat16)).astype(jnp.float32)
    block_acc = jnp.einsum('bhqk,bkhd->bqhd', rounded, values.astype(jnp.float32))
    return (block_max, block_sum, block_acc)

def merge_blocks(member, block_max, block_sum, block_acc):
    chosen = member[:, :, None, None]
    group_max = lax.optimization_barrier(jnp.max(jnp.where(chosen, block_max[None], NEGATIVE_FILL), axis=1))
    scale_all = jnp.where(chosen, jnp.exp(block_max[None] - group_max[:, None]), 0.0)
    group_sum = lax.optimization_barrier(jnp.sum(scale_all * block_sum[None], axis=1))
    group_acc = jnp.einsum('gshq,sqhd->gqhd', scale_all, block_acc, precision=lax.Precision.HIGHEST)
    present = group_sum > 0.0
    safe_sum = jnp.where(present, group_sum, 1.0)
    present_t = jnp.swapaxes(present, 1, 2)[..., None]
    out_values = jnp.where(present_t, group_acc / jnp.swapaxes(safe_sum, 1, 2)[..., None], 0.0).astype(jnp.bfloat16)
    group_lse = jnp.where(present, group_max + jnp.log(safe_sum), NEGATIVE_FILL)
    return (out_values, jnp.swapaxes(group_lse, 1, 2))

def reference(hidden_in, router_choice, w_router, w_kv, w_query, w_out, kv_cache, page_count, tail_len, page_perm, parents, accepted_leaf):
    split_count = N_EXP // EXPERTS
    head_width = KVH * HD
    part_width = w_query.shape[2]
    scale_factor = HD ** (-0.5)
    tokens = hidden_in.reshape(-1, D).astype(jnp.float32)
    normed = (tokens * lax.rsqrt(lax.optimization_barrier(jnp.mean(tokens * tokens, axis=-1, keepdims=True)) + NORM_EPSILON)).astype(jnp.bfloat16)
    logits = jnp.dot(normed, w_router, preferred_element_type=jnp.float32)
    picked = router_choice.reshape(-1, TOPK)
    gate_values = jax.nn.softmax(jnp.take_along_axis(logits, picked, axis=1), axis=-1)
    reachable = ancestry(parents)
    depth_of = (lax.optimization_barrier(jnp.sum(reachable, axis=-1)) - 1.0).astype(jnp.int32)
    lengths = (page_count - 1) * PAGE + tail_len
    positions = lengths[..., None] + depth_of
    projected = jnp.dot(normed, w_kv, preferred_element_type=jnp.float32).reshape(N_EXP, GREQ, DRAFT, 2, KVH, HD)
    new_keys = rotate(projected[..., 0, :, :], positions).astype(jnp.bfloat16)
    new_values = projected[..., 1, :, :].astype(jnp.bfloat16)
    new_kv = jnp.concatenate([new_keys.reshape(N_EXP, GREQ, DRAFT, head_width), new_values.reshape(N_EXP, GREQ, DRAFT, head_width)], axis=-1)
    rows_dev = REQ_X * DRAFT
    row_total = tokens.shape[0]
    block_count = row_total // rows_dev
    pair_experts = picked.reshape(block_count, rows_dev * TOPK)
    onehot = (pair_experts[..., None] == jnp.arange(EXPERTS, dtype=jnp.int32)).astype(jnp.int32)
    slot_rank = lax.optimization_barrier(jnp.sum((jnp.cumsum(onehot, axis=1).astype(jnp.int32) - onehot) * onehot, axis=-1)).astype(jnp.int32)
    target = ((pair_experts * block_count + jnp.arange(block_count, dtype=jnp.int32)[:, None]) * CAP + slot_rank).reshape(-1).astype(jnp.int32)
    pair_total = target.shape[0]
    buffer_size = EXPERTS * block_count * CAP
    source = jnp.full((buffer_size,), pair_total, jnp.int32).at[target].set(jnp.arange(pair_total, dtype=jnp.int32))
    row_source = jnp.where(source == pair_total, row_total, source // TOPK).astype(jnp.int32)
    padded_rows = jnp.concatenate([normed, jnp.zeros((1, D), jnp.bfloat16)], axis=0)
    routed_rows = padded_rows[row_source].reshape(EXPERTS, block_count * CAP, D)
    query_weights = w_query.reshape(EXPERTS, split_count, D, part_width).transpose(0, 2, 1, 3).reshape(EXPERTS, D, head_width)

    def project_queries(item_pair):
        return jnp.dot(item_pair[0], item_pair[1], preferred_element_type=jnp.float32).astype(jnp.bfloat16)
    query_buffer = lax.map(project_queries, (routed_rows, query_weights))
    raw_queries = query_buffer.reshape(buffer_size, head_width)[target].reshape(N_EXP, GREQ, DRAFT, TOPK, KVH, HD)
    queries = rotate(raw_queries.astype(jnp.float32), positions[..., None]).astype(jnp.bfloat16)
    ends = jnp.cumsum(page_count, axis=-1).astype(jnp.int32)
    starts = ends - page_count
    page_index = jnp.arange(MAXP, dtype=jnp.int32)
    page_valid = page_index < page_count[..., None]
    global_page = jnp.where(page_valid, starts[..., None] + page_index, 0).astype(jnp.int32)
    column_ids = jnp.broadcast_to(jnp.arange(N_EXP, dtype=jnp.int32)[:, None, None], global_page.shape)
    slot_ids = page_perm[column_ids, global_page]
    holders = slot_ids // SLOTS
    column_of = jnp.broadcast_to(jnp.arange(N_EXP, dtype=jnp.int32)[:, None], (N_EXP, GREQ))
    request_total = N_EXP * GREQ
    holder_ids = jnp.arange(N_REQ, dtype=jnp.int32)

    def attend(item_set):
        query_one, key_new, value_new, reach_one, slot_one, valid_one, holder_one, length_one, column_one = item_set
        page_blocks = kv_cache[column_one, slot_one]
        page_keys = page_blocks[..., :head_width].reshape(MAXP, PAGE, KVH, HD)
        page_values = page_blocks[..., head_width:].reshape(MAXP, PAGE, KVH, HD)
        query_wide = query_one.astype(jnp.float32)
        scores = jnp.einsum('qhd,pkhd->phqk', query_wide, page_keys.astype(jnp.float32)) * scale_factor
        key_pos = page_index[:, None] * PAGE + jnp.arange(PAGE, dtype=jnp.int32)
        key_valid = valid_one[:, None] & (key_pos < length_one)
        page_max, page_sum, page_acc = block_partial(scores, key_valid[:, None, None, :], page_values)
        holder_member = valid_one[None, :] & (holder_one[None, :] == holder_ids[:, None])
        holder_out, holder_lse = merge_blocks(holder_member, page_max, page_sum, page_acc)
        tree_scores = jnp.einsum('qhd,khd->hqk', query_wide, key_new.astype(jnp.float32)) * scale_factor
        tree_valid = jnp.repeat(reach_one, TOPK, axis=0) > 0.5
        tree_max, tree_sum, tree_acc = block_partial(tree_scores[None], tree_valid[None, None], value_new[None])
        tree_out, tree_lse = merge_blocks(jnp.ones((1, 1), bool), tree_max, tree_sum, tree_acc)
        all_lse = jnp.concatenate([holder_lse, tree_lse], axis=0)
        all_out = jnp.concatenate([holder_out, tree_out], axis=0).astype(jnp.float32)
        top_lse = lax.optimization_barrier(jnp.max(all_lse, axis=0))
        part_weight = jnp.exp(all_lse - top_lse)
        mixed_out = lax.optimization_barrier(jnp.sum(part_weight[..., None] * all_out, axis=0)) / lax.optimization_barrier(jnp.sum(part_weight, axis=0))[..., None]
        return mixed_out.astype(jnp.bfloat16)
    item_set = (queries.reshape(request_total, DRAFT * TOPK, KVH, HD), new_keys.reshape(request_total, DRAFT, KVH, HD), new_values.reshape(request_total, DRAFT, KVH, HD), reachable.reshape(request_total, DRAFT, DRAFT), slot_ids.reshape(request_total, MAXP), page_valid.reshape(request_total, MAXP), holders.reshape(request_total, MAXP), lengths.reshape(request_total), column_of.reshape(request_total))
    attended = lax.map(attend, item_set)
    attended_pairs = attended.reshape(pair_total, head_width)
    padded_pairs = jnp.concatenate([attended_pairs, jnp.zeros((1, head_width), jnp.bfloat16)], axis=0)
    routed_out = padded_pairs[source].reshape(EXPERTS, block_count * CAP, split_count, part_width)
    out_weights = w_out.reshape(EXPERTS, split_count, part_width, D)

    def project_out(item_pair):
        return jnp.einsum('rsh,shd->rsd', item_pair[0].astype(jnp.float32), item_pair[1].astype(jnp.float32)).astype(jnp.bfloat16)
    out_buffer = lax.map(project_out, (routed_out, out_weights))
    pair_out = lax.optimization_barrier(jnp.sum(out_buffer.reshape(buffer_size, split_count, D)[target].astype(jnp.float32), axis=1))
    combined = lax.optimization_barrier(jnp.sum(pair_out.reshape(row_total, TOPK, D) * gate_values[..., None], axis=1))
    attn_out = combined.astype(jnp.bfloat16).reshape(N_EXP, GREQ, DRAFT, D)
    leaf_row = jnp.take_along_axis(reachable, accepted_leaf[..., None, None].astype(jnp.int32), axis=2)[..., 0, :]
    selector = leaf_row[..., None, :] * (depth_of[..., None, :] == jnp.arange(DRAFT, dtype=jnp.int32)[:, None]).astype(jnp.float32)
    cache_rows = jnp.einsum('xgdj,xgjc->xgdc', selector, new_kv.astype(jnp.float32)).astype(jnp.bfloat16)
    return (attn_out, cache_rows)
```

```python
import jax
import jax.numpy as jnp
from jax import lax
from jax.experimental import pallas as pl
from jax.experimental.pallas import tpu as pltpu
from jax.sharding import PartitionSpec as P

D = 2048
HD = 128
EXPERTS = 8
KVH = 8
TOPK = 2
PAGE = 128
DRAFT = 64
REQ_X = 2
SLOTS = 16
CAP = 48
ROWS = REQ_X * DRAFT
QROWS = DRAFT * TOPK
HEADW = KVH * HD
BUF = EXPERTS * CAP

NEGATIVE_FILL = -1e30
NORM_EPSILON = 1e-06
SCALE = HD**-0.5
LOG2E = 1.4426950408889634
EXP_SCALE = SCALE * LOG2E
F32 = jnp.float32
BF16 = jnp.bfloat16
VMEM = pltpu.VMEM


def whole(shape):
    return pl.BlockSpec(shape, lambda *_: (0,) * len(shape))


def rotate_head(x, cos_full, sin_full):
    return x * cos_full + pltpu.roll(x, HD // 2, 1) * sin_full


def prologue_kernel(hidden_ref, choice_ref, choice_t_ref, router_ref, routed_ref, normed_ref, gates_ref, slots_ref):
    tokens = hidden_ref[...].astype(F32)
    mean_sq = jnp.mean(tokens * tokens, axis=-1, keepdims=True)
    normed = (tokens * lax.rsqrt(mean_sq + NORM_EPSILON)).astype(BF16)
    normed_ref[...] = normed
    logits = jnp.dot(normed, router_ref[...], preferred_element_type=F32)
    lane8 = lax.broadcasted_iota(jnp.int32, (ROWS, EXPERTS), 1)
    hot = [lane8 == choice_ref[:, t : t + 1] for t in range(TOPK)]
    picked = [jnp.sum(jnp.where(h, logits, 0.0), axis=1, keepdims=True) for h in hot]
    top = jnp.maximum(picked[0], picked[1])
    raised = [jnp.exp(p - top) for p in picked]
    total = raised[0] + raised[1]
    row_i = lax.broadcasted_iota(jnp.int32, (ROWS, ROWS), 0)
    col_i = lax.broadcasted_iota(jnp.int32, (ROWS, ROWS), 1)
    lower = (col_i < row_i).astype(F32).astype(BF16)
    both = (hot[0] | hot[1]).astype(F32).astype(BF16)
    before = jnp.dot(lower, both, preferred_element_type=F32)
    for t in range(TOPK):
        gates_ref[:, t : t + 1] = raised[t] / total
        rank = jnp.sum(jnp.where(hot[t], before, 0.0), axis=1, keepdims=True)
        slots_ref[:, t : t + 1] = choice_ref[:, t : t + 1] * CAP + rank.astype(jnp.int32)
    sub8 = lax.broadcasted_iota(jnp.int32, (EXPERTS, ROWS), 0)
    hot_t = [sub8 == choice_t_ref[t : t + 1, :] for t in range(TOPK)]
    upper = (row_i < col_i).astype(F32).astype(BF16)
    both_t = (hot_t[0] | hot_t[1]).astype(F32).astype(BF16)
    before_t = jnp.dot(both_t, upper, preferred_element_type=F32)
    slot_row = [
        choice_t_ref[t : t + 1, :] * CAP
        + jnp.sum(jnp.where(hot_t[t], before_t, 0.0), axis=0, keepdims=True).astype(jnp.int32)
        for t in range(TOPK)
    ]
    buf_i = lax.broadcasted_iota(jnp.int32, (BUF, ROWS), 0)
    spread = ((buf_i == slot_row[0]) | (buf_i == slot_row[1])).astype(F32).astype(BF16)
    for n in range(D // 512):
        cols = slice(n * 512, (n + 1) * 512)
        routed_ref[:, cols] = jnp.dot(spread, normed[:, cols], preferred_element_type=F32).astype(BF16)


def prologue(hidden, choice, w_router):
    return pl.pallas_call(
        prologue_kernel,
        out_shape=(
            jax.ShapeDtypeStruct((BUF, D), BF16),
            jax.ShapeDtypeStruct((ROWS, D), BF16),
            jax.ShapeDtypeStruct((ROWS, TOPK), F32),
            jax.ShapeDtypeStruct((ROWS, TOPK), jnp.int32),
        ),
        name="prologue",
    )(hidden, choice, choice.T, w_router)


def expert_query_kernel(parity_ref, rows_ref, own_ref, other_ref, out_ref):
    n = pl.program_id(0)

    @pl.when(n < 2)
    def _():
        out_ref[...] = jnp.dot(rows_ref[...], own_ref[...], preferred_element_type=F32).astype(BF16)

    @pl.when(n >= 2)
    def _():
        out_ref[...] = jnp.dot(rows_ref[...], other_ref[...], preferred_element_type=F32).astype(BF16)


def expert_query(parity, rows, w_own, w_other):
    width = w_own.shape[1] // 2
    return pl.pallas_call(
        expert_query_kernel,
        out_shape=jax.ShapeDtypeStruct((BUF, HEADW), BF16),
        grid_spec=pltpu.PrefetchScalarGridSpec(
            num_scalar_prefetch=1,
            grid=(4,),
            in_specs=[
                pl.BlockSpec((BUF, D), lambda n, par: (0, 0)),
                pl.BlockSpec((D, width), lambda n, par: (0, jnp.minimum(n, 1))),
                pl.BlockSpec((D, width), lambda n, par: (0, jnp.maximum(n - 2, 0))),
            ],
            out_specs=pl.BlockSpec(
                (BUF, width),
                lambda n, par: (0, jnp.where(n < 2, par[0] * 2 + n, (1 - par[0]) * 2 + n - 2)),
            ),
        ),
        name="expert_query",
    )(parity, rows, w_own, w_other)


def pick_rotate_kernel(slots_ref, cos_ref, sin_ref, back_ref, out_ref):
    buf_i = lax.broadcasted_iota(jnp.int32, (ROWS, BUF), 1)
    for t in range(TOPK):
        pick = (buf_i == slots_ref[:, t : t + 1]).astype(F32).astype(BF16)
        for h in range(KVH):
            cols = slice(h * HD, (h + 1) * HD)
            raw = jnp.dot(pick, back_ref[:, cols], preferred_element_type=F32)
            turned = rotate_head(raw, cos_ref[...], sin_ref[...]).astype(BF16)
            for r in range(REQ_X):
                out_ref[r, t * DRAFT : (t + 1) * DRAFT, cols] = turned[r * DRAFT : (r + 1) * DRAFT]


def pick_rotate(slots, cos_full, sin_full, back):
    return pl.pallas_call(
        pick_rotate_kernel,
        out_shape=jax.ShapeDtypeStruct((REQ_X, QROWS, HEADW), BF16),
        name="pick_rotate",
    )(slots, cos_full, sin_full, back)


def new_kv_kernel(normed_ref, weight_ref, cos_ref, sin_ref, out_ref):
    tile = jnp.dot(normed_ref[...], weight_ref[...], preferred_element_type=F32)
    n = pl.program_id(0)
    is_key = n < pl.num_programs(0) // 2

    @pl.when(is_key)
    def _():
        for h in range(tile.shape[1] // HD):
            cols = slice(h * HD, (h + 1) * HD)
            out_ref[:, cols] = rotate_head(tile[:, cols], cos_ref[...], sin_ref[...]).astype(BF16)

    @pl.when(jnp.logical_not(is_key))
    def _():
        out_ref[...] = tile.astype(BF16)


def project_kv(normed, w_kv, cos_full, sin_full):
    tile = 512
    return pl.pallas_call(
        new_kv_kernel,
        out_shape=jax.ShapeDtypeStruct((ROWS, 2 * HEADW), BF16),
        grid=(2 * HEADW // tile,),
        in_specs=[
            whole((ROWS, D)),
            pl.BlockSpec((D, tile), lambda n: (0, n)),
            whole((ROWS, HD)),
            whole((ROWS, HD)),
        ],
        out_specs=pl.BlockSpec((ROWS, tile), lambda n: (0, n)),
        cost_estimate=pl.CostEstimate(flops=2 * ROWS * D * D, bytes_accessed=2 * D * D, transcendentals=0),
        name="project_kv",
    )(normed, w_kv, cos_full, sin_full)


def columns_to_rows(columns):
    lane = lax.broadcasted_iota(jnp.int32, (QROWS, HD), 1)
    wide = jnp.zeros((QROWS, HD), F32)
    for h, column in enumerate(columns):
        wide = jnp.where(lane == h, column, wide)
    return wide.T[:KVH]


def page_kernel(order_ref, request_ref, valid_ref, query_ref, cache_ref, out_ref, lse_ref, max_ref, sum_ref, acc_ref):
    i = pl.program_id(0)
    last_i = pl.num_programs(0) - 1
    here = request_ref[i]
    starts = (i == 0) | (request_ref[jnp.maximum(i - 1, 0)] != here)
    finishes = (i == last_i) | (request_ref[jnp.minimum(i + 1, last_i)] != here)

    @pl.when(i == 0)
    def _():
        lse_ref[...] = jnp.full_like(lse_ref, NEGATIVE_FILL)

    @pl.when(starts)
    def _():
        max_ref[...] = jnp.full_like(max_ref, NEGATIVE_FILL)
        sum_ref[...] = jnp.zeros_like(sum_ref)
        acc_ref[...] = jnp.zeros_like(acc_ref)

    lane = lax.broadcasted_iota(jnp.int32, (QROWS, PAGE), 1)
    valid = lane < valid_ref[i]
    for h in range(KVH):
        cols = slice(h * HD, (h + 1) * HD)
        scores = lax.dot_general(
            query_ref[0, :, cols], cache_ref[0, :, cols], (((1,), (1,)), ((), ())), preferred_element_type=F32
        )
        scores = jnp.where(valid, scores, NEGATIVE_FILL)
        page_max = jnp.max(scores, axis=-1, keepdims=True)
        weights = jnp.exp2((scores - page_max) * EXP_SCALE)
        page_sum = jnp.sum(weights, axis=-1, keepdims=True)
        page_acc = jnp.dot(
            weights.astype(BF16), cache_ref[0, :, HEADW + h * HD : HEADW + (h + 1) * HD], preferred_element_type=F32
        )
        old_max = max_ref[h]
        new_max = jnp.maximum(old_max, page_max)
        old_scale = jnp.exp2((old_max - new_max) * EXP_SCALE)
        page_scale = jnp.exp2((page_max - new_max) * EXP_SCALE)
        max_ref[h] = new_max
        sum_ref[h] = sum_ref[h] * old_scale + page_sum * page_scale
        acc_ref[:, cols] = acc_ref[:, cols] * old_scale + page_acc * page_scale

    @pl.when(finishes)
    def _():
        columns = []
        for h in range(KVH):
            cols = slice(h * HD, (h + 1) * HD)
            total = sum_ref[h]
            out_ref[0, :, cols] = (acc_ref[:, cols] / total).astype(BF16)
            columns.append(max_ref[h] * SCALE + jnp.log(total))
        lse_ref[here] = columns_to_rows(columns)


def attend_pages(order, requests, valid, queries, cache):
    count = queries.shape[0]
    return pl.pallas_call(
        page_kernel,
        out_shape=(
            jax.ShapeDtypeStruct((count, QROWS, HEADW), BF16),
            jax.ShapeDtypeStruct((count, KVH, QROWS), F32),
        ),
        grid_spec=pltpu.PrefetchScalarGridSpec(
            num_scalar_prefetch=3,
            grid=(SLOTS,),
            in_specs=[
                pl.BlockSpec((1, QROWS, HEADW), lambda i, o, r, v: (r[i], 0, 0)),
                pl.BlockSpec((1, PAGE, 2 * HEADW), lambda i, o, r, v: (o[i], 0, 0)),
            ],
            out_specs=(
                pl.BlockSpec((1, QROWS, HEADW), lambda i, o, r, v: (r[i], 0, 0)),
                pl.BlockSpec((count, KVH, QROWS), lambda i, o, r, v: (0, 0, 0)),
            ),
            scratch_shapes=[VMEM((KVH, QROWS, 1), F32), VMEM((KVH, QROWS, 1), F32), VMEM((QROWS, HEADW), F32)],
        ),
        name="attend_pages",
    )(order, requests, valid, queries, cache)


def tree_kernel(query_ref, kv_ref, reach_ref, out_ref, lse_ref):
    for r in range(REQ_X):
        rows = slice(r * DRAFT, (r + 1) * DRAFT)
        reach = reach_ref[r]
        valid = jnp.concatenate([reach] * TOPK, axis=0) > 0.5
        columns = []
        for h in range(KVH):
            cols = slice(h * HD, (h + 1) * HD)
            scores = lax.dot_general(
                query_ref[r, :, cols], kv_ref[rows, cols], (((1,), (1,)), ((), ())), preferred_element_type=F32
            )
            scores = jnp.where(valid, scores, NEGATIVE_FILL)
            top = jnp.max(scores, axis=-1, keepdims=True)
            weights = jnp.exp2((scores - top) * EXP_SCALE)
            total = jnp.sum(weights, axis=-1, keepdims=True)
            acc = jnp.dot(
                weights.astype(BF16), kv_ref[rows, HEADW + h * HD : HEADW + (h + 1) * HD], preferred_element_type=F32
            )
            out_ref[r, :, cols] = (acc / total).astype(BF16)
            columns.append(top * SCALE + jnp.log(total))
        lse_ref[r] = columns_to_rows(columns)


def attend_tree(queries, new_kv, reachable):
    return pl.pallas_call(
        tree_kernel,
        out_shape=(
            jax.ShapeDtypeStruct((REQ_X, QROWS, HEADW), BF16),
            jax.ShapeDtypeStruct((REQ_X, KVH, QROWS), F32),
        ),
        cost_estimate=pl.CostEstimate(flops=10**9, bytes_accessed=10**6, transcendentals=10**5),
        name="attend_tree",
    )(queries, new_kv, reachable)


def mix_kernel(slots_ref, home_ref, home_lse_ref, tree_ref, tree_lse_ref, out_ref, mixed_ref):
    holders = home_ref.shape[0]
    for r in range(REQ_X):
        lses = [home_lse_ref[p, r] for p in range(holders)] + [tree_lse_ref[r]]
        top = lses[0]
        for lse in lses[1:]:
            top = jnp.maximum(top, lse)
        raised = [jnp.exp(lse - top) for lse in lses]
        total = raised[0]
        for one in raised[1:]:
            total = total + one
        shares = jnp.concatenate(raised + [total] * (HD // KVH - holders - 1), axis=0).T
        for h in range(KVH):
            cols = slice(h * HD, (h + 1) * HD)
            mixed = tree_ref[r, :, cols].astype(F32) * shares[:, holders * KVH + h : holders * KVH + h + 1]
            for p in range(holders):
                share = shares[:, p * KVH + h : p * KVH + h + 1]
                mixed = mixed + jnp.where(share > 0.0, home_ref[p, r, :, cols].astype(F32) * share, 0.0)
            whole_sum = shares[:, (holders + 1) * KVH + h : (holders + 1) * KVH + h + 1]
            mixed = (mixed / whole_sum).astype(BF16)
            for t in range(TOPK):
                start = t * ROWS + r * DRAFT
                mixed_ref[start : start + DRAFT, cols] = mixed[t * DRAFT : (t + 1) * DRAFT]
    buf_i = lax.broadcasted_iota(jnp.int32, (ROWS, BUF), 1)
    placed = None
    for t in range(TOPK):
        pick = (buf_i == slots_ref[:, t : t + 1]).astype(F32).astype(BF16)
        part = lax.dot_general(
            pick, mixed_ref[t * ROWS : (t + 1) * ROWS, :], (((0,), (0,)), ((), ())), preferred_element_type=F32
        )
        placed = part if placed is None else placed + part
    out_ref[...] = placed.astype(BF16)


def mix(slots, home_out, home_lse, tree_out, tree_lse):
    return pl.pallas_call(
        mix_kernel,
        out_shape=jax.ShapeDtypeStruct((BUF, HEADW), BF16),
        scratch_shapes=[VMEM((TOPK * ROWS, HEADW), BF16)],
        name="mix",
    )(slots, home_out, home_lse, tree_out, tree_lse)


def expert_out_kernel(parity_ref, mine_ref, theirs_ref, own_ref, other_ref, out_ref):
    total = jnp.dot(mine_ref[...], own_ref[...], preferred_element_type=F32)
    total = total + jnp.dot(theirs_ref[...], other_ref[...], preferred_element_type=F32)
    out_ref[...] = total.astype(BF16)


def expert_out(parity, rows, w_own, w_other):
    depth = w_own.shape[0]
    tile = 512
    return pl.pallas_call(
        expert_out_kernel,
        out_shape=jax.ShapeDtypeStruct((BUF, D), BF16),
        grid_spec=pltpu.PrefetchScalarGridSpec(
            num_scalar_prefetch=1,
            grid=(D // tile,),
            in_specs=[
                pl.BlockSpec((BUF, depth), lambda n, par: (0, par[0])),
                pl.BlockSpec((BUF, depth), lambda n, par: (0, 1 - par[0])),
                pl.BlockSpec((depth, tile), lambda n, par: (0, n)),
                pl.BlockSpec((depth, tile), lambda n, par: (0, n)),
            ],
            out_specs=pl.BlockSpec((BUF, tile), lambda n, par: (0, n)),
        ),
        name="expert_out",
    )(parity, rows, rows, w_own, w_other)


def combine_kernel(slots_ref, gates_ref, back_ref, out_ref):
    buf_i = lax.broadcasted_iota(jnp.int32, (ROWS, BUF), 1)
    total = None
    for t in range(TOPK):
        pick = (buf_i == slots_ref[:, t : t + 1]).astype(F32).astype(BF16)
        part = jnp.dot(pick, back_ref[...], preferred_element_type=F32) * gates_ref[:, t : t + 1]
        total = part if total is None else total + part
    out_ref[...] = total.astype(BF16)


def combine(slots, gates, back):
    tile = 512
    return pl.pallas_call(
        combine_kernel,
        out_shape=jax.ShapeDtypeStruct((ROWS, D), BF16),
        grid=(D // tile,),
        in_specs=[whole((ROWS, TOPK)), whole((ROWS, TOPK)), pl.BlockSpec((BUF, tile), lambda n: (0, n))],
        out_specs=pl.BlockSpec((ROWS, tile), lambda n: (0, n)),
        name="combine",
    )(slots, gates, back)


def ancestry(parent_ids):
    count_tokens = parent_ids.shape[-1]
    index_row = jnp.arange(count_tokens, dtype=jnp.int32)
    linked = (parent_ids[..., :, None] == index_row) & (index_row[:, None] > 0)
    reachable = (linked | (index_row[:, None] == index_row)).astype(BF16)
    for doubling in range(count_tokens.bit_length() - 1):
        reachable = jnp.minimum(jnp.matmul(reachable, reachable, preferred_element_type=F32), 1.0).astype(BF16)
    return reachable.astype(F32)


def partner_half(weight):
    count = lax.axis_size("req")
    rows = weight.shape[0] // count
    piece = lax.dynamic_slice_in_dim(weight, lax.axis_index("req") * rows, rows)
    piece = lax.ppermute(piece, "exp", [(i, i ^ 1) for i in range(lax.axis_size("exp"))])
    return lax.all_gather(piece, "req", axis=0, tiled=True)


def exchange(rows):
    return lax.all_to_all(rows, "exp", split_axis=0, concat_axis=0, tiled=True)


def body(
    hidden_in,
    router_choice,
    w_router,
    w_kv,
    w_query,
    w_out,
    kv_cache,
    page_count,
    tail_len,
    page_perm,
    parents,
    accepted_leaf,
):
    holder_count = lax.axis_size("req")
    owner_index = lax.axis_index("req")
    parity = (lax.axis_index("exp") % 2).astype(jnp.int32).reshape(1)
    group_requests = page_count.shape[1]
    pool_size = page_perm.shape[1]

    query_other = partner_half(w_query[0])
    out_other = partner_half(w_out[0])

    choice = router_choice.reshape(ROWS, TOPK)
    routed, normed, gates, slots = prologue(hidden_in.reshape(ROWS, D), choice, w_router)
    arrived = exchange(routed)
    query_back = exchange(expert_query(parity, arrived, w_query[0], query_other))

    reachable = ancestry(parents[0])
    depth_of = (jnp.sum(reachable, axis=-1) - 1.0).astype(jnp.int32)
    counts_all = page_count[0]
    lengths_all = (counts_all - 1) * PAGE + tail_len[0]
    own_lengths = lax.dynamic_slice_in_dim(lengths_all, owner_index * REQ_X, REQ_X)
    positions = (own_lengths[:, None] + depth_of).reshape(ROWS)
    half = HD // 2
    inverse_freq = 10000.0 ** (-jnp.arange(half, dtype=F32) / half)
    angles = positions.astype(F32)[:, None] * inverse_freq
    cosine, sine = jnp.cos(angles), jnp.sin(angles)
    cos_full = jnp.concatenate([cosine, cosine], axis=-1)
    sin_full = jnp.concatenate([-sine, sine], axis=-1)
    new_kv = project_kv(normed, w_kv, cos_full, sin_full)

    queries = pick_rotate(slots, cos_full, sin_full, query_back)
    shared = lax.all_gather(queries, "req", axis=0, tiled=True)

    ends = jnp.cumsum(counts_all)
    starts = ends - counts_all
    mine = owner_index * SLOTS + jnp.arange(SLOTS, dtype=jnp.int32)
    found = page_perm[0][None, :] == mine[:, None]
    page_pos = jnp.sum(jnp.where(found, jnp.arange(pool_size, dtype=jnp.int32)[None, :], 0), axis=1)
    slot_rank = jnp.sum((page_pos[None, :] < page_pos[:, None]).astype(jnp.int32), axis=1)
    slot_i = jnp.arange(SLOTS, dtype=jnp.int32)
    sorted_hot = slot_rank[None, :] == slot_i[:, None]
    order = jnp.sum(jnp.where(sorted_hot, slot_i[None, :], 0), axis=1)
    sorted_pos = jnp.sum(jnp.where(sorted_hot, page_pos[None, :], 0), axis=1)
    sorted_request = jnp.sum((ends[None, :] <= sorted_pos[:, None]).astype(jnp.int32), axis=1)
    member = sorted_request[:, None] == jnp.arange(group_requests, dtype=jnp.int32)[None, :]
    remaining = jnp.sum(jnp.where(member, (lengths_all + starts * PAGE)[None, :], 0), axis=1)
    sorted_valid = remaining - sorted_pos * PAGE

    held_out, held_lse = attend_pages(order, sorted_request, sorted_valid, shared, kv_cache[0])
    home_out = lax.all_to_all(
        held_out.reshape(holder_count, REQ_X, QROWS, HEADW), "req", split_axis=0, concat_axis=0, tiled=True
    )
    home_lse = lax.all_to_all(
        held_lse.reshape(holder_count, REQ_X, KVH, QROWS), "req", split_axis=0, concat_axis=0, tiled=True
    )
    tree_out, tree_lse = attend_tree(queries, new_kv, reachable)
    placed = mix(slots, home_out, home_lse, tree_out, tree_lse)
    out_back = exchange(expert_out(parity, exchange(placed), w_out[0], out_other))
    attn_out = combine(slots, gates, out_back).reshape(1, REQ_X, DRAFT, D)

    token_i = jnp.arange(DRAFT, dtype=jnp.int32)
    leaf_hot = accepted_leaf[0][:, None] == token_i[None, :]
    leaf_row = jnp.sum(jnp.where(leaf_hot[:, :, None], reachable, 0.0), axis=1)
    selector = (leaf_row[:, None, :] * (depth_of[:, None, :] == token_i[:, None]).astype(F32)).astype(BF16)
    cache_rows = jnp.einsum(
        "rdj,rjc->rdc", selector, new_kv.reshape(REQ_X, DRAFT, 2 * HEADW), preferred_element_type=F32
    ).astype(BF16)[None]
    return (attn_out, cache_rows)


def solution(mesh):
    placed = (
        P("exp", "req", None, None),
        P("exp", "req", None, None),
        P(),
        P(),
        P("exp", None, None),
        P("exp", None, None),
        P("exp", "req", None, None),
        P("exp", None),
        P("exp", None),
        P("exp", None),
        P("exp", "req", None),
        P("exp", "req"),
    )
    return jax.shard_map(
        body,
        mesh=mesh,
        in_specs=placed,
        out_specs=(P("exp", "req", None, None), P("exp", "req", None, None)),
        check_vma=False,
    )
```

```python
import jax
import jax.numpy as jnp
from jax import lax
from jax.experimental import pallas as pl
from jax.experimental.pallas import tpu as pltpu
from jax.sharding import PartitionSpec as P

D = 2048
HD = 128
EXPERTS = 8
KVH = 8
TOPK = 2
PAGE = 128
DRAFT = 64
REQ_X = 2
SLOTS = 16
CAP = 48
ROWS = REQ_X * DRAFT
QROWS = DRAFT * TOPK
HEADW = KVH * HD
BUF = EXPERTS * CAP

NEGATIVE_FILL = -1e30
NORM_EPSILON = 1e-06
SCALE = HD**-0.5
LOG2E = 1.4426950408889634
EXP_SCALE = SCALE * LOG2E
F32 = jnp.float32
BF16 = jnp.bfloat16
VMEM = pltpu.VMEM
DMA = pltpu.SemaphoreType.DMA
MESH = pl.DeviceIdType.MESH
ABSENT = -1e29


def whole(shape):
    return pl.BlockSpec(shape, lambda *_: (0,) * len(shape))


def rotate_head(x, cos_full, sin_full):
    return x * cos_full + pltpu.roll(x, HD // 2, 1) * sin_full


def prologue_kernel(hidden_ref, choice_ref, choice_t_ref, router_ref, routed_ref, normed_ref, gates_ref, slots_ref, slot_rows_ref):
    tokens = hidden_ref[...].astype(F32)
    mean_sq = jnp.mean(tokens * tokens, axis=-1, keepdims=True)
    normed = (tokens * lax.rsqrt(mean_sq + NORM_EPSILON)).astype(BF16)
    normed_ref[...] = normed
    logits = jnp.dot(normed, router_ref[...], preferred_element_type=F32)
    lane8 = lax.broadcasted_iota(jnp.int32, (ROWS, EXPERTS), 1)
    hot = [lane8 == choice_ref[:, t : t + 1] for t in range(TOPK)]
    picked = [jnp.sum(jnp.where(h, logits, 0.0), axis=1, keepdims=True) for h in hot]
    top = jnp.maximum(picked[0], picked[1])
    raised = [jnp.exp(p - top) for p in picked]
    total = raised[0] + raised[1]
    row_i = lax.broadcasted_iota(jnp.int32, (ROWS, ROWS), 0)
    col_i = lax.broadcasted_iota(jnp.int32, (ROWS, ROWS), 1)
    lower = (col_i < row_i).astype(F32).astype(BF16)
    both = (hot[0] | hot[1]).astype(F32).astype(BF16)
    before = jnp.dot(lower, both, preferred_element_type=F32)
    for t in range(TOPK):
        gates_ref[:, t : t + 1] = raised[t] / total
        rank = jnp.sum(jnp.where(hot[t], before, 0.0), axis=1, keepdims=True)
        slots_ref[:, t : t + 1] = choice_ref[:, t : t + 1] * CAP + rank.astype(jnp.int32)
    sub8 = lax.broadcasted_iota(jnp.int32, (EXPERTS, ROWS), 0)
    hot_t = [sub8 == choice_t_ref[t : t + 1, :] for t in range(TOPK)]
    upper = (row_i < col_i).astype(F32).astype(BF16)
    both_t = (hot_t[0] | hot_t[1]).astype(F32).astype(BF16)
    before_t = jnp.dot(both_t, upper, preferred_element_type=F32)
    slot_row = [
        choice_t_ref[t : t + 1, :] * CAP
        + jnp.sum(jnp.where(hot_t[t], before_t, 0.0), axis=0, keepdims=True).astype(jnp.int32)
        for t in range(TOPK)
    ]
    for r in range(REQ_X):
        lanes = slice(r * DRAFT, (r + 1) * DRAFT)
        slot_rows_ref[r : r + 1, :] = jnp.concatenate([row[:, lanes] for row in slot_row], axis=1)
    buf_i = lax.broadcasted_iota(jnp.int32, (BUF, ROWS), 0)
    spread = ((buf_i == slot_row[0]) | (buf_i == slot_row[1])).astype(F32).astype(BF16)
    for n in range(D // 512):
        cols = slice(n * 512, (n + 1) * 512)
        routed_ref[:, cols] = jnp.dot(spread, normed[:, cols], preferred_element_type=F32).astype(BF16)


def prologue(hidden, choice, w_router):
    return pl.pallas_call(
        prologue_kernel,
        out_shape=(
            jax.ShapeDtypeStruct((BUF, D), BF16),
            jax.ShapeDtypeStruct((ROWS, D), BF16),
            jax.ShapeDtypeStruct((ROWS, TOPK), F32),
            jax.ShapeDtypeStruct((ROWS, TOPK), jnp.int32),
            jax.ShapeDtypeStruct((REQ_X, QROWS), jnp.int32),
        ),
        name="prologue",
    )(hidden, choice, choice.T, w_router)


def expert_query_kernel(parity_ref, rows_ref, own_ref, other_ref, out_ref):
    n = pl.program_id(0)

    @pl.when(n < 2)
    def _():
        out_ref[...] = jnp.dot(rows_ref[...], own_ref[...], preferred_element_type=F32).astype(BF16)

    @pl.when(n >= 2)
    def _():
        out_ref[...] = jnp.dot(rows_ref[...], other_ref[...], preferred_element_type=F32).astype(BF16)


def expert_query(parity, rows, w_own, w_other):
    width = w_own.shape[1] // 2
    return pl.pallas_call(
        expert_query_kernel,
        out_shape=jax.ShapeDtypeStruct((BUF, HEADW), BF16),
        grid_spec=pltpu.PrefetchScalarGridSpec(
            num_scalar_prefetch=1,
            grid=(4,),
            in_specs=[
                pl.BlockSpec((BUF, D), lambda n, par: (0, 0)),
                pl.BlockSpec((D, width), lambda n, par: (0, jnp.minimum(n, 1))),
                pl.BlockSpec((D, width), lambda n, par: (0, jnp.maximum(n - 2, 0))),
            ],
            out_specs=pl.BlockSpec(
                (BUF, width),
                lambda n, par: (0, jnp.where(n < 2, par[0] * 2 + n, (1 - par[0]) * 2 + n - 2)),
            ),
        ),
        name="expert_query",
    )(parity, rows, w_own, w_other)


def pick_rotate_kernel(slots_ref, cos_ref, sin_ref, back_ref, out_ref):
    buf_i = lax.broadcasted_iota(jnp.int32, (ROWS, BUF), 1)
    for t in range(TOPK):
        pick = (buf_i == slots_ref[:, t : t + 1]).astype(F32).astype(BF16)
        for h in range(KVH):
            cols = slice(h * HD, (h + 1) * HD)
            raw = jnp.dot(pick, back_ref[:, cols], preferred_element_type=F32)
            turned = rotate_head(raw, cos_ref[...], sin_ref[...]).astype(BF16)
            for r in range(REQ_X):
                out_ref[r, t * DRAFT : (t + 1) * DRAFT, cols] = turned[r * DRAFT : (r + 1) * DRAFT]


def pick_rotate(slots, cos_full, sin_full, back):
    return pl.pallas_call(
        pick_rotate_kernel,
        out_shape=jax.ShapeDtypeStruct((REQ_X, QROWS, HEADW), BF16),
        name="pick_rotate",
    )(slots, cos_full, sin_full, back)


def new_kv_kernel(normed_ref, weight_ref, cos_ref, sin_ref, out_ref):
    tile = jnp.dot(normed_ref[...], weight_ref[...], preferred_element_type=F32)
    n = pl.program_id(0)
    is_key = n < pl.num_programs(0) // 2

    @pl.when(is_key)
    def _():
        for h in range(tile.shape[1] // HD):
            cols = slice(h * HD, (h + 1) * HD)
            out_ref[:, cols] = rotate_head(tile[:, cols], cos_ref[...], sin_ref[...]).astype(BF16)

    @pl.when(jnp.logical_not(is_key))
    def _():
        out_ref[...] = tile.astype(BF16)


def project_kv(normed, w_kv, cos_full, sin_full):
    tile = 512
    return pl.pallas_call(
        new_kv_kernel,
        out_shape=jax.ShapeDtypeStruct((ROWS, 2 * HEADW), BF16),
        grid=(2 * HEADW // tile,),
        in_specs=[
            whole((ROWS, D)),
            pl.BlockSpec((D, tile), lambda n: (0, n)),
            whole((ROWS, HD)),
            whole((ROWS, HD)),
        ],
        out_specs=pl.BlockSpec((ROWS, tile), lambda n: (0, n)),
        cost_estimate=pl.CostEstimate(flops=2 * ROWS * D * D, bytes_accessed=2 * D * D, transcendentals=0),
        name="project_kv",
    )(normed, w_kv, cos_full, sin_full)


def block_attention(keys, values, queries, valid):
    scores = lax.dot_general(keys, queries, (((1,), (1,)), ((), ())), preferred_element_type=F32)
    scores = jnp.where(valid, scores, NEGATIVE_FILL)
    top = jnp.max(scores, axis=0, keepdims=True)
    weights = jnp.exp2((scores - top) * EXP_SCALE)
    total = jnp.sum(weights, axis=0, keepdims=True)
    acc = lax.dot_general(values, weights.astype(BF16), (((0,), (0,)), ((), ())), preferred_element_type=F32)
    return top, total, acc


def head_rows(h):
    return slice(h * HD, (h + 1) * HD)


def value_cols(h):
    return slice(HEADW + h * HD, HEADW + (h + 1) * HD)


def page_kernel(order_ref, request_ref, valid_ref, query_ref, cache_ref, out_ref, lse_ref, max_ref, sum_ref, acc_ref):
    i = pl.program_id(0)
    last_i = pl.num_programs(0) - 1
    here = request_ref[i]
    starts = (i == 0) | (request_ref[jnp.maximum(i - 1, 0)] != here)
    finishes = (i == last_i) | (request_ref[jnp.minimum(i + 1, last_i)] != here)

    @pl.when(i == 0)
    def _():
        lse_ref[...] = jnp.full_like(lse_ref, NEGATIVE_FILL)

    @pl.when(starts)
    def _():
        max_ref[...] = jnp.full_like(max_ref, NEGATIVE_FILL)
        sum_ref[...] = jnp.zeros_like(sum_ref)
        acc_ref[...] = jnp.zeros_like(acc_ref)

    valid = lax.broadcasted_iota(jnp.int32, (PAGE, QROWS), 0) < valid_ref[i]
    for h in range(KVH):
        rows = head_rows(h)
        page_max, page_sum, page_acc = block_attention(
            cache_ref[0, :, rows], cache_ref[0, :, value_cols(h)], query_ref[0, :, rows], valid
        )
        old_max = max_ref[h : h + 1]
        new_max = jnp.maximum(old_max, page_max)
        old_scale = jnp.exp2((old_max - new_max) * EXP_SCALE)
        page_scale = jnp.exp2((page_max - new_max) * EXP_SCALE)
        max_ref[h : h + 1] = new_max
        sum_ref[h : h + 1] = sum_ref[h : h + 1] * old_scale + page_sum * page_scale
        acc_ref[rows] = acc_ref[rows] * old_scale + page_acc * page_scale

    @pl.when(finishes)
    def _():
        total = sum_ref[...]
        for h in range(KVH):
            out_ref[0, head_rows(h)] = (acc_ref[head_rows(h)] / total[h : h + 1]).astype(BF16)
        lse_ref[here] = max_ref[...] * SCALE + jnp.log(total)


def attend_pages(order, requests, valid, queries, cache):
    count = queries.shape[0]
    return pl.pallas_call(
        page_kernel,
        out_shape=(
            jax.ShapeDtypeStruct((count, HEADW, QROWS), BF16),
            jax.ShapeDtypeStruct((count, KVH, QROWS), F32),
        ),
        grid_spec=pltpu.PrefetchScalarGridSpec(
            num_scalar_prefetch=3,
            grid=(SLOTS,),
            in_specs=[
                pl.BlockSpec((1, QROWS, HEADW), lambda i, o, r, v: (r[i], 0, 0)),
                pl.BlockSpec((1, PAGE, 2 * HEADW), lambda i, o, r, v: (o[i], 0, 0)),
            ],
            out_specs=(
                pl.BlockSpec((1, HEADW, QROWS), lambda i, o, r, v: (r[i], 0, 0)),
                pl.BlockSpec((count, KVH, QROWS), lambda i, o, r, v: (0, 0, 0)),
            ),
            scratch_shapes=[VMEM((KVH, QROWS), F32), VMEM((KVH, QROWS), F32), VMEM((HEADW, QROWS), F32)],
        ),
        name="attend_pages",
    )(order, requests, valid, queries, cache)


def shares_of(lses):
    top = lses[0]
    for lse in lses[1:]:
        top = jnp.maximum(top, lse)
    raised = [jnp.exp(lse - top) for lse in lses]
    total = raised[0]
    for one in raised[1:]:
        total = total + one
    return [one / total for one in raised], top + jnp.log(total)


def merge_parts(parts, store):
    shares, lse = shares_of([part[1] for part in parts])
    for h in range(KVH):
        rows = head_rows(h)
        merged = None
        for (ref, part_lse, raw), share in zip(parts, shares):
            values = ref[rows].astype(F32)
            if raw:
                values = jnp.where(part_lse[h : h + 1] > ABSENT, values, 0.0)
            values = values * share[h : h + 1]
            merged = values if merged is None else merged + values
        store(rows, merged.astype(BF16))
    return lse


def home_kernel(
    out_ref, lse_ref, query_ref, kv_ref, reach_ref, slot_rows_ref, placed_ref,
    sib_buf, sib_lse, send_buf, send_lse, recv_buf, recv_lse, tree_buf, mixed_buf,
    sib_send, sib_recv, ring_send, ring_recv,
):
    me = lax.axis_index("req")
    count = lax.axis_size("req")
    chips = count // 2
    core, chip = me % 2, me // 2
    sibling = chip * 2 + 1 - core
    after = ((chip + 1) % chips) * 2 + core
    before = ((chip + chips - 1) % chips) * 2 + core
    barrier = pltpu.get_barrier_semaphore()
    for peer in (sibling, after, before):
        pl.semaphore_signal(barrier, inc=1, device_id={"req": peer}, device_id_type=MESH)
    pl.semaphore_wait(barrier, 3)

    def copy(src, dst, send, recv, peer):
        one = pltpu.make_async_remote_copy(
            src_ref=src, dst_ref=dst, send_sem=send, recv_sem=recv, device_id={"req": peer}, device_id_type=MESH
        )
        one.start()
        return one

    owners = [(chip + off) % chips for off in (2, 1, 3, 0)]
    mine = [(owner * 2 + core) * REQ_X for owner in owners]
    sib_copies = []
    for k, owner in enumerate(owners):
        theirs = (owner * 2 + 1 - core) * REQ_X
        sib_copies.append([
            copy(lse_ref.at[pl.ds(theirs, REQ_X)], sib_lse.at[k], sib_send.at[2 * k], sib_recv.at[2 * k], sibling),
            copy(out_ref.at[pl.ds(theirs, REQ_X)], sib_buf.at[k], sib_send.at[2 * k + 1], sib_recv.at[2 * k + 1], sibling),
        ])

    tree_lses = []
    for r in range(REQ_X):
        tokens = slice(r * DRAFT, (r + 1) * DRAFT)
        valid = reach_ref[r] > 0.5
        tops, totals = [], []
        for h in range(KVH):
            top, total, acc = block_attention(
                kv_ref[tokens, head_rows(h)], kv_ref[tokens, value_cols(h)], query_ref[r, :, head_rows(h)], valid
            )
            tree_buf[r, head_rows(h)] = (acc / total).astype(BF16)
            tops.append(top)
            totals.append(total)
        tree_lses.append(jnp.concatenate(tops, axis=0) * SCALE + jnp.log(jnp.concatenate(totals, axis=0)))

    def chip_parts(k, r):
        return [
            (out_ref.at[mine[k] + r], lse_ref[mine[k] + r], True),
            (sib_buf.at[k, r], sib_lse[k, r], True),
        ]

    def relay(slot, parts, peer):
        def store(rows, values):
            send_buf[slot, rows] = values

        send_lse[slot] = merge_parts(parts, store)
        return [
            copy(send_lse.at[slot], recv_lse.at[slot], ring_send.at[2 * slot], ring_recv.at[2 * slot], peer),
            copy(send_buf.at[slot], recv_buf.at[slot], ring_send.at[2 * slot + 1], ring_recv.at[2 * slot + 1], peer),
        ]

    def arrive(copies):
        for one in copies:
            one.wait_recv()

    def came(slot):
        return (recv_buf.at[slot], recv_lse[slot], False)

    ring = [None] * 6
    arrive(sib_copies[0])
    ring[0] = relay(0, chip_parts(0, 0), after)
    ring[1] = relay(1, chip_parts(0, 1), before)
    arrive(sib_copies[1])
    ring[2] = relay(2, chip_parts(1, 1), after)
    arrive(sib_copies[2])
    ring[3] = relay(3, chip_parts(2, 0), before)
    arrive(ring[0])
    ring[4] = relay(4, chip_parts(1, 0) + [came(0)], after)
    arrive(ring[1])
    ring[5] = relay(5, chip_parts(2, 1) + [came(1)], before)
    arrive(sib_copies[3])

    buf_i = lax.broadcasted_iota(jnp.int32, (BUF, QROWS), 0)
    total = None
    for slot in (2, 3, 4, 5):
        arrive(ring[slot])
    for r in range(REQ_X):
        parts = chip_parts(3, r) + [came(s) for s in ((4, 3), (2, 5))[r]]
        parts.append((tree_buf.at[r], tree_lses[r], False))

        def store(rows, values):
            mixed_buf[r, rows] = values

        merge_parts(parts, store)
    for n in range(2):
        cols = slice(n * HEADW // 2, (n + 1) * HEADW // 2)
        total = None
        for r in range(REQ_X):
            spread = (buf_i == slot_rows_ref[r : r + 1, :]).astype(F32).astype(BF16)
            part = lax.dot_general(spread, mixed_buf[r, cols], (((1,), (1,)), ((), ())), preferred_element_type=F32)
            total = part if total is None else total + part
        placed_ref[:, cols] = total.astype(BF16)
    for copies in sib_copies + ring:
        for one in copies:
            one.wait_send()


def bring_home(held_out, held_lse, queries, new_kv, reach_t, slot_rows):
    chips = held_out.shape[0] // REQ_X // 2
    part = (HEADW, QROWS)
    rows = (KVH, QROWS)
    return pl.pallas_call(
        home_kernel,
        out_shape=jax.ShapeDtypeStruct((BUF, HEADW), BF16),
        scratch_shapes=[
            VMEM((chips, REQ_X) + part, BF16),
            VMEM((chips, REQ_X) + rows, F32),
            VMEM((6,) + part, BF16),
            VMEM((6,) + rows, F32),
            VMEM((6,) + part, BF16),
            VMEM((6,) + rows, F32),
            VMEM((REQ_X,) + part, BF16),
            VMEM((REQ_X,) + part, BF16),
            DMA((2 * chips,)),
            DMA((2 * chips,)),
            DMA((12,)),
            DMA((12,)),
        ],
        compiler_params=pltpu.CompilerParams(collective_id=0, has_side_effects=True),
        name="bring_home",
    )(held_out, held_lse, queries, new_kv, reach_t, slot_rows)


def expert_out_kernel(parity_ref, mine_ref, theirs_ref, own_ref, other_ref, out_ref):
    total = jnp.dot(mine_ref[...], own_ref[...], preferred_element_type=F32)
    total = total + jnp.dot(theirs_ref[...], other_ref[...], preferred_element_type=F32)
    out_ref[...] = total.astype(BF16)


def expert_out(parity, rows, w_own, w_other):
    depth = w_own.shape[0]
    tile = 512
    return pl.pallas_call(
        expert_out_kernel,
        out_shape=jax.ShapeDtypeStruct((BUF, D), BF16),
        grid_spec=pltpu.PrefetchScalarGridSpec(
            num_scalar_prefetch=1,
            grid=(D // tile,),
            in_specs=[
                pl.BlockSpec((BUF, depth), lambda n, par: (0, par[0])),
                pl.BlockSpec((BUF, depth), lambda n, par: (0, 1 - par[0])),
                pl.BlockSpec((depth, tile), lambda n, par: (0, n)),
                pl.BlockSpec((depth, tile), lambda n, par: (0, n)),
            ],
            out_specs=pl.BlockSpec((BUF, tile), lambda n, par: (0, n)),
        ),
        name="expert_out",
    )(parity, rows, rows, w_own, w_other)


def combine_kernel(slots_ref, gates_ref, back_ref, out_ref):
    buf_i = lax.broadcasted_iota(jnp.int32, (ROWS, BUF), 1)
    total = None
    for t in range(TOPK):
        pick = (buf_i == slots_ref[:, t : t + 1]).astype(F32).astype(BF16)
        part = jnp.dot(pick, back_ref[...], preferred_element_type=F32) * gates_ref[:, t : t + 1]
        total = part if total is None else total + part
    out_ref[...] = total.astype(BF16)


def combine(slots, gates, back):
    tile = 512
    return pl.pallas_call(
        combine_kernel,
        out_shape=jax.ShapeDtypeStruct((ROWS, D), BF16),
        grid=(D // tile,),
        in_specs=[whole((ROWS, TOPK)), whole((ROWS, TOPK)), pl.BlockSpec((BUF, tile), lambda n: (0, n))],
        out_specs=pl.BlockSpec((ROWS, tile), lambda n: (0, n)),
        name="combine",
    )(slots, gates, back)


def ancestry(parent_ids):
    count_tokens = parent_ids.shape[-1]
    index_row = jnp.arange(count_tokens, dtype=jnp.int32)
    linked = (parent_ids[..., :, None] == index_row) & (index_row[:, None] > 0)
    reachable = (linked | (index_row[:, None] == index_row)).astype(BF16)
    for doubling in range(count_tokens.bit_length() - 1):
        reachable = jnp.minimum(jnp.matmul(reachable, reachable, preferred_element_type=F32), 1.0).astype(BF16)
    return reachable.astype(F32)


def partner_half(weight):
    count = lax.axis_size("req")
    rows = weight.shape[0] // count
    piece = lax.dynamic_slice_in_dim(weight, lax.axis_index("req") * rows, rows)
    piece = lax.ppermute(piece, "exp", [(i, i ^ 1) for i in range(lax.axis_size("exp"))])
    return lax.all_gather(piece, "req", axis=0, tiled=True)


def exchange(rows):
    return lax.all_to_all(rows, "exp", split_axis=0, concat_axis=0, tiled=True)


def body(
    hidden_in,
    router_choice,
    w_router,
    w_kv,
    w_query,
    w_out,
    kv_cache,
    page_count,
    tail_len,
    page_perm,
    parents,
    accepted_leaf,
):
    owner_index = lax.axis_index("req")
    parity = (lax.axis_index("exp") % 2).astype(jnp.int32).reshape(1)
    group_requests = page_count.shape[1]
    pool_size = page_perm.shape[1]

    query_other = partner_half(w_query[0])
    out_other = partner_half(w_out[0])

    choice = router_choice.reshape(ROWS, TOPK)
    routed, normed, gates, slots, slot_rows = prologue(hidden_in.reshape(ROWS, D), choice, w_router)
    arrived = exchange(routed)
    query_back = exchange(expert_query(parity, arrived, w_query[0], query_other))

    reachable = ancestry(parents[0])
    depth_of = (jnp.sum(reachable, axis=-1) - 1.0).astype(jnp.int32)
    counts_all = page_count[0]
    lengths_all = (counts_all - 1) * PAGE + tail_len[0]
    own_lengths = lax.dynamic_slice_in_dim(lengths_all, owner_index * REQ_X, REQ_X)
    positions = (own_lengths[:, None] + depth_of).reshape(ROWS)
    half = HD // 2
    inverse_freq = 10000.0 ** (-jnp.arange(half, dtype=F32) / half)
    angles = positions.astype(F32)[:, None] * inverse_freq
    cosine, sine = jnp.cos(angles), jnp.sin(angles)
    cos_full = jnp.concatenate([cosine, cosine], axis=-1)
    sin_full = jnp.concatenate([-sine, sine], axis=-1)
    new_kv = project_kv(normed, w_kv, cos_full, sin_full)

    queries = pick_rotate(slots, cos_full, sin_full, query_back)
    shared = lax.all_gather(queries, "req", axis=0, tiled=True)

    ends = jnp.cumsum(counts_all)
    starts = ends - counts_all
    mine = owner_index * SLOTS + jnp.arange(SLOTS, dtype=jnp.int32)
    found = page_perm[0][None, :] == mine[:, None]
    page_pos = jnp.sum(jnp.where(found, jnp.arange(pool_size, dtype=jnp.int32)[None, :], 0), axis=1)
    slot_rank = jnp.sum((page_pos[None, :] < page_pos[:, None]).astype(jnp.int32), axis=1)
    slot_i = jnp.arange(SLOTS, dtype=jnp.int32)
    sorted_hot = slot_rank[None, :] == slot_i[:, None]
    order = jnp.sum(jnp.where(sorted_hot, slot_i[None, :], 0), axis=1)
    sorted_pos = jnp.sum(jnp.where(sorted_hot, page_pos[None, :], 0), axis=1)
    sorted_request = jnp.sum((ends[None, :] <= sorted_pos[:, None]).astype(jnp.int32), axis=1)
    member = sorted_request[:, None] == jnp.arange(group_requests, dtype=jnp.int32)[None, :]
    remaining = jnp.sum(jnp.where(member, (lengths_all + starts * PAGE)[None, :], 0), axis=1)
    sorted_valid = remaining - sorted_pos * PAGE

    held_out, held_lse = attend_pages(order, sorted_request, sorted_valid, shared, kv_cache[0])
    reach_t = jnp.swapaxes(reachable, 1, 2)
    reach_t = jnp.concatenate([reach_t] * TOPK, axis=-1)
    placed = bring_home(held_out, held_lse, queries, new_kv, reach_t, slot_rows)
    out_back = exchange(expert_out(parity, exchange(placed), w_out[0], out_other))
    attn_out = combine(slots, gates, out_back).reshape(1, REQ_X, DRAFT, D)

    token_i = jnp.arange(DRAFT, dtype=jnp.int32)
    leaf_hot = accepted_leaf[0][:, None] == token_i[None, :]
    leaf_row = jnp.sum(jnp.where(leaf_hot[:, :, None], reachable, 0.0), axis=1)
    selector = (leaf_row[:, None, :] * (depth_of[:, None, :] == token_i[:, None]).astype(F32)).astype(BF16)
    cache_rows = jnp.einsum(
        "rdj,rjc->rdc", selector, new_kv.reshape(REQ_X, DRAFT, 2 * HEADW), preferred_element_type=F32
    ).astype(BF16)[None]
    return (attn_out, cache_rows)


def solution(mesh):
    placed = (
        P("exp", "req", None, None),
        P("exp", "req", None, None),
        P(),
        P(),
        P("exp", None, None),
        P("exp", None, None),
        P("exp", "req", None, None),
        P("exp", None),
        P("exp", None),
        P("exp", None),
        P("exp", "req", None),
        P("exp", "req"),
    )
    return jax.shard_map(
        body,
        mesh=mesh,
        in_specs=placed,
        out_specs=(P("exp", "req", None, None), P("exp", "req", None, None)),
        check_vma=False,
    )
```

```python
import jax
import jax.numpy as jnp
import numpy as np
from jax import lax
from jax.experimental import pallas as pl
from jax.experimental.pallas import tpu as pltpu
from jax.sharding import PartitionSpec as P

D = 2048
HD = 128
EXPERTS = 8
KVH = 8
TOPK = 2
PAGE = 128
DRAFT = 64
REQ_X = 2
SLOTS = 16
CAP = 48
ROWS = REQ_X * DRAFT
QROWS = DRAFT * TOPK
HEADW = KVH * HD
BUF = EXPERTS * CAP
HALFH = KVH // 2
HALFW = HEADW // 2
GROUP = 2
SIDE = 4
CHUNKS = 4
PARTS = 2

NEGATIVE_FILL = -1e30
NORM_EPSILON = 1e-06
SCALE = HD**-0.5
LOG2E = 1.4426950408889634
EXP_SCALE = SCALE * LOG2E
F32 = jnp.float32
BF16 = jnp.bfloat16
VMEM = pltpu.VMEM
DMA = pltpu.SemaphoreType.DMA
MESH = pl.DeviceIdType.MESH
ABSENT = -1e29


def rotate_head(x, cos_full, sin_full):
    return x * cos_full + pltpu.roll(x, HD // 2, 1) * sin_full


def send_to(src, dst, send, recv, axis, peer):
    return pltpu.make_async_remote_copy(
        src_ref=src, dst_ref=dst, send_sem=send, recv_sem=recv, device_id={axis: peer}, device_id_type=MESH
    )


def req_places():
    me = lax.axis_index("req")
    chips = lax.axis_size("req") // 2
    core, chip = me % 2, me // 2
    after, before, across = (chip + 1) % chips, (chip + chips - 1) % chips, (chip + 2) % chips
    return core, chip, after, before, across


def expert_peer(k, back=False):
    place = lax.axis_index("exp")
    x, y = place % SIDE, place // SIDE
    rows_on = (y + (SIDE - k % SIDE if back else k % SIDE)) % SIDE
    return rows_on * SIDE + (SIDE - 1 - x if k >= SIDE else x)


def group_slots(first, lanes):
    place = lax.axis_index("exp")
    x, y = place % SIDE, place // SIDE
    column = SIDE - 1 - x if first >= SIDE else x
    row = iota((GROUP * CAP, lanes), 0)
    step = (row >= CAP).astype(jnp.int32)
    to = y + first % SIDE + step
    to = jnp.where(to >= SIDE, to - SIDE, to)
    return (2 * to + column // 2 - step) * CAP + row


class RoundTrip:
    def __init__(self, sems, refs, parts_out, parts_back, prepare, work, use):
        self.there_send, self.there_recv, self.back_send, self.back_recv = sems
        self.rows_ref, self.arrived_ref, self.result_ref, self.back_ref = refs
        self.parts_out, self.parts_back = parts_out, parts_back
        self.prepare, self.work, self.use = prepare, work, use
        self.me, self.count, self.rows = lax.axis_index("exp") // 2, EXPERTS, CAP
        self.groups = range(0, self.count, GROUP)
        self.out_copies, self.home_copies, self.keeps, self.stays = {}, [], [], []

    def block(self, index):
        return pl.ds(pl.multiple_of(index * self.rows, 8), self.rows)

    def group_rows(self, first):
        return slice(first * self.rows, (first + GROUP) * self.rows)

    def columns(self, ref, parts, part):
        width = ref.shape[1] // parts
        return slice(part * width, (part + 1) * width)

    def homeward(self, k, part, lands):
        cols = self.columns(self.back_ref, self.parts_back, part)
        slot = part * self.count + k
        return send_to(
            self.result_ref.at[self.block(k), cols], self.back_ref.at[self.block(lands), cols],
            self.back_send.at[slot], self.back_recv.at[slot], "exp", expert_peer(k, back=True),
        )

    def send(self, part, ready=None):
        cols = self.columns(self.rows_ref, self.parts_out, part)
        for first in self.groups:
            self.prepare(first, self.group_rows(first), part)
            if first == 0 and ready is not None:
                ready()
            for k in range(first, first + GROUP):
                src, dst = self.rows_ref.at[self.block(k), cols], self.arrived_ref.at[self.block(k), cols]
                slot = part * self.count + k
                if k == 0:
                    one = pltpu.make_async_copy(src, dst, self.there_recv.at[slot])
                    self.keeps.append(one)
                else:
                    one = send_to(src, dst, self.there_send.at[slot], self.there_recv.at[slot], "exp", expert_peer(k))
                    self.out_copies[slot] = one
                one.start()

    def send_back(self, first, part):
        for k in range(first, first + GROUP):
            if k == 0:
                cols = self.columns(self.back_ref, self.parts_back, part)
                one = pltpu.make_async_copy(
                    self.result_ref.at[self.block(0), cols], self.back_ref.at[self.block(self.me), cols],
                    self.back_recv.at[part * self.count],
                )
                self.stays.append(one)
            else:
                one = self.homeward(k, part, self.me)
                self.home_copies.append(one)
            one.start()

    def run(self):
        last = self.count - GROUP
        for first in self.groups:
            if first == last:
                for part in range(1, self.parts_back):
                    for early in self.groups[:-1]:
                        self.work(self.group_rows(early), part)
            for k in range(first, first + GROUP):
                for part in range(self.parts_out):
                    if k == 0:
                        self.keeps[part].wait()
                    else:
                        self.out_copies[part * self.count + k].wait_recv()
            self.work(self.group_rows(first), 0)
            self.send_back(first, 0)
        for part in range(1, self.parts_back):
            for first in self.groups[:-1]:
                self.send_back(first, part)
            self.work(self.group_rows(last), part)
            self.send_back(last, part)
        for part in range(self.parts_back):
            self.stays[part].wait()
            for k in range(1, self.count):
                self.homeward(k, part, expert_peer(k) // 2).wait_recv()
            self.use(part)

    def drain(self):
        for one in list(self.out_copies.values()) + self.home_copies:
            one.wait_send()


class Gather:
    SLOTS = 14

    def __init__(self, view, send, recv):
        self.view, self.send, self.recv = view, send, recv
        core, chip, after, before, across = req_places()
        same = [place * 2 + core for place in (chip, after, before, across)]
        other = [place * 2 + 1 - core for place in (chip, after, before, across)]
        self.own, self.after, self.before, self.across = same
        self.sibling = other[0]
        table = []
        for h in range(2):
            table.append((self.after, self.own, h, self.before))
        for h in range(2):
            table.append((self.before, self.own, h, self.after))
        for h in range(2):
            table.append((self.sibling, self.own, h, other[0]))
        table.append((self.after, self.before, 0, self.across))
        table.append((self.before, self.after, 1, self.across))
        for here, there in ((self.before, other[2]), (self.after, other[1]), (self.across, other[3])):
            for h in range(2):
                table.append((self.sibling, here, h, there))
        self.table = table
        self.started = []

    def start(self, slot, source=None):
        peer, block, half, _ = self.table[slot]
        place = self.view(block, half)
        one = send_to(place if source is None else source, place, self.send.at[slot], self.recv.at[slot], "req", peer)
        one.start()
        self.started.append(one)

    def arrive(self, slot):
        peer, _, half, block = self.table[slot]
        place = self.view(block, half)
        send_to(place, place, self.send.at[slot], self.recv.at[slot], "req", peer).wait_recv()

    def send_own(self, half, source=None):
        for slot in (half, 2 + half, 4 + half):
            self.start(slot, source)

    def relay(self):
        for came, onward in ((0, (6, 8)), (3, (7, 11)), (1, (9,)), (2, (10,))):
            self.arrive(came)
            for slot in onward:
                self.start(slot)

    def relay_across(self):
        for came, onward in ((6, 12), (7, 13)):
            self.arrive(came)
            self.start(onward)

    def finish(self):
        for slot in (4, 5, 8, 9, 10, 11, 12, 13):
            self.arrive(slot)
        for one in self.started:
            one.wait_send()


def one_hot(mask):
    return mask.astype(F32).astype(BF16)


def iota(shape, dim):
    return lax.broadcasted_iota(jnp.int32, shape, dim)


def lane_sum(mask, values):
    return jnp.sum(jnp.where(mask, values, 0.0), axis=1, keepdims=True)


def row_sum(mask, values):
    return jnp.sum(jnp.where(mask, values, 0.0), axis=0, keepdims=True)


def page_table(counts, tails, perm):
    me = lax.axis_index("req")
    requests, pool = counts.shape[1], perm.shape[1]
    g_row, g_col = iota((requests, requests), 0), iota((requests, requests), 1)
    ends = lane_sum(g_col <= g_row, counts)
    last_key = (ends - 1.0) * PAGE + lane_sum(g_col == g_row, tails)
    page = iota((requests, pool), 1).astype(F32)
    request = jnp.minimum(jnp.sum((ends <= page).astype(F32), axis=0, keepdims=True), requests - 1.0)
    valid = row_sum(iota((requests, pool), 0).astype(F32) == request, last_key) - page[:1] * PAGE
    slot = perm - (me * SLOTS).astype(F32)
    held = (slot >= 0.0) & (slot < float(SLOTS))
    earlier = one_hot(iota((pool, pool), 0) < iota((pool, pool), 1))
    rank = jnp.dot(
        jnp.broadcast_to(one_hot(held), (8, pool)), earlier, preferred_element_type=F32
    )[:1]
    hit = held & (rank == iota((SLOTS, pool), 0).astype(F32))
    columns = [lane_sum(hit, values) for values in (slot, request, valid)]
    each = iota((requests, pool), 0).astype(F32)
    upto = lane_sum(held & (request <= each), jnp.ones_like(request))
    columns.append(jnp.clip(upto - 1.0, 0.0, SLOTS - 1.0))
    columns.append(lane_sum(held & (request == each), jnp.ones_like(request)))
    columns = [column.astype(jnp.int32) for column in columns]
    for n in (0, 1, 3):
        columns[n] = jnp.clip(columns[n], 0, SLOTS - 1)
    return columns


def query_stage(
    hidden_ref, choice_ref, router_ref, counts_ref, tails_ref, perm_ref, parents_ref, leaf_ref, freq_ref,
    query_hbm, kv_hbm, query_bufs, cache_ref,
    kv_ref, reach_ref, gates_ref, slots_ref, slot_rows_ref, table_wide, table_ref, mine_ref,
    normed_ref, routed_ref, arrived_ref, result_ref, back_ref, halves_ref, weight_ref,
    cos_ref, sin_ref, depth_ref,
    load_sem, there_send, there_recv, back_send, back_recv, piece_send, piece_recv,
    wq_send, wq_recv, q_send, q_recv, enter,
):
    place = lax.axis_index("exp")
    me, count = lax.axis_index("req"), lax.axis_size("req")
    parity = place % 2
    partner = place + 1 - 2 * parity
    loads = [
        pltpu.make_async_copy(query_hbm, halves_ref.at[parity], load_sem.at[0]),
        pltpu.make_async_copy(kv_hbm, weight_ref, load_sem.at[1]),
    ]
    for load in loads:
        load.start()

    tokens = hidden_ref[...].astype(F32)
    mean_sq = jnp.mean(tokens * tokens, axis=-1, keepdims=True)
    normed_ref[...] = (tokens * lax.rsqrt(mean_sq + NORM_EPSILON)).astype(BF16)
    choice_row = [
        jnp.concatenate([choice_ref[r, t : t + 1] for r in range(REQ_X)], axis=1) for t in range(TOPK)
    ]
    hot_t = [iota((EXPERTS, ROWS), 0) == row for row in choice_row]
    upper = one_hot(iota((ROWS, ROWS), 0) < iota((ROWS, ROWS), 1))
    earlier = jnp.dot(one_hot(hot_t[0] | hot_t[1]), upper, preferred_element_type=F32)
    slot_row = [row.astype(F32) * CAP + row_sum(hot, earlier) for row, hot in zip(choice_row, hot_t)]
    slot_int = [row.astype(jnp.int32) for row in slot_row]
    piece_rows = query_hbm.shape[0] // count // 2

    def piece_place(block, half):
        return pl.ds(pl.multiple_of((2 * block + half) * piece_rows, 8), piece_rows)

    def query_view(block, half):
        return halves_ref.at[1 - parity, piece_place(block, half)]

    pieces = [
        send_to(
            query_hbm.at[piece_place(me, half)], halves_ref.at[parity, piece_place(me, half)],
            piece_send.at[half], piece_recv.at[half], "exp", partner,
        )
        for half in range(2)
    ]

    def prepare(first, rows, _):
        slot = group_slots(first, ROWS)
        spread = one_hot((slot == slot_int[0]) | (slot == slot_int[1]))
        for n in range(D // 512):
            cols = slice(n * 512, (n + 1) * 512)
            routed_ref[rows, cols] = jnp.dot(spread, normed_ref[:, cols], preferred_element_type=F32).astype(BF16)

    def ready():
        enter()
        for piece in pieces:
            piece.start()

    def await_piece(half):
        place_here = query_view(me, half)
        send_to(place_here, place_here, piece_send.at[half], piece_recv.at[half], "exp", partner).wait_recv()

    to_scalars = pltpu.make_async_copy(table_wide, table_ref, load_sem.at[6])

    def meanwhile():
        ring = Gather(query_view, wq_send, wq_recv)
        for half in range(2):
            await_piece(half)
            ring.send_own(half)
        logits = lax.dot_general(
            router_ref[...], normed_ref[...], (((1,), (1,)), ((), ())), preferred_element_type=F32
        )
        picked = [row_sum(hot, logits) for hot in hot_t]
        top = jnp.maximum(picked[0], picked[1])
        raised = [jnp.exp(one - top) for one in picked]
        total = raised[0] + raised[1]
        wide = jnp.concatenate(
            [one / total for one in raised] + slot_row + [jnp.zeros((ROWS - 2 * TOPK, ROWS), F32)], axis=0
        ).T
        gates_ref[...] = wide[:, :TOPK]
        slots_ref[...] = wide[:, TOPK : 2 * TOPK].astype(jnp.int32)
        for r in range(REQ_X):
            lanes = slice(r * DRAFT, (r + 1) * DRAFT)
            slot_rows_ref[r : r + 1, :] = jnp.concatenate([row[:, lanes] for row in slot_int], axis=1)
        counts, tails = counts_ref[...].astype(F32), tails_ref[...].astype(F32)
        lane = iota(table_wide.shape, 1)
        table = jnp.zeros(table_wide.shape, jnp.int32)
        for n, column in enumerate(page_table(counts, tails, perm_ref[...].astype(F32))):
            table = jnp.where(lane == n, column, table)
        table_wide[...] = table
        to_scalars.start()
        sub, lane = iota((DRAFT, DRAFT), 0), iota((DRAFT, DRAFT), 1)
        seen = [
            one_hot(((sub == parents_ref[r : r + 1, :]) & (lane > 0)) | (sub == lane)) for r in range(REQ_X)
        ]
        for doubling in range(DRAFT.bit_length() - 1):
            seen = [
                jnp.minimum(jnp.dot(one, one, preferred_element_type=F32), 1.0).astype(BF16) for one in seen
            ]
        lengths = (counts - 1.0) * PAGE + tails
        request_lane = iota(lengths.shape, 1)
        for r in range(REQ_X):
            depth = lax.dot_general(
                seen[r], jnp.ones((DRAFT, HD), BF16), (((0,), (0,)), ((), ())), preferred_element_type=F32
            ) - 1.0
            depth_ref[r] = depth
            wide_seen = seen[r].astype(F32)
            reach_ref[r] = jnp.concatenate([wide_seen] * TOPK, axis=1)
            length = lane_sum(request_lane == me * REQ_X + r, lengths)
            angles = (depth + length) * freq_ref[...]
            rows = slice(r * DRAFT, (r + 1) * DRAFT)
            sine = jnp.sin(angles)
            cos_ref[rows] = jnp.cos(angles)
            sin_ref[rows] = jnp.where(iota((DRAFT, HD), 1) < HD // 2, -sine, sine)
        ring.relay()

        loads[1].wait()
        for n in range(2 * HEADW // 256):
            cols = slice(n * 256, (n + 1) * 256)
            tile = jnp.dot(normed_ref[...], weight_ref[:, cols], preferred_element_type=F32)
            for h in range(2):
                head = tile[:, h * HD : (h + 1) * HD]
                if n < HEADW // 256:
                    head = rotate_head(head, cos_ref[...], sin_ref[...])
                kv_ref[:, n * 256 + h * HD : n * 256 + (h + 1) * HD] = head.astype(BF16)
        ring.relay_across()
        token_lane = iota((DRAFT, DRAFT), 1)
        for r in range(REQ_X):
            on_path = lane_sum(token_lane == leaf_ref[:, r : r + 1], reach_ref[r][:, :DRAFT])
            depth_lane = iota((DRAFT, HD), 1).astype(F32) == depth_ref[r]
            chosen = one_hot(depth_lane & (on_path > 0.5))[:, :DRAFT]
            rows = slice(r * DRAFT, (r + 1) * DRAFT)
            for n in range(4):
                cols = slice(n * 512, (n + 1) * 512)
                cache_ref[rows, cols] = lax.dot_general(
                    chosen, kv_ref[rows, cols], (((0,), (0,)), ((), ())), preferred_element_type=F32
                ).astype(BF16)
        loads[0].wait()
        ring.finish()

    def project(rows, part):
        for n in range(2):
            weight_cols = slice(n * 256, (n + 1) * 256)
            cols = slice(part * 512 + n * 256, part * 512 + (n + 1) * 256)
            result_ref[rows, cols] = jnp.dot(
                arrived_ref[rows], halves_ref[part, :, weight_cols], preferred_element_type=F32
            ).astype(BF16)

    buf_cols = iota((DRAFT, BUF), 1)
    keeps, rings = [], []

    def turn(part):
        cols = slice(part * 512, (part + 1) * 512)

        def request_view(block, half):
            return query_bufs[part].at[block * REQ_X + half]

        ring = Gather(request_view, q_send.at[part], q_recv.at[part])
        rings.append(ring)
        for r in range(REQ_X):
            rows = slice(r * DRAFT, (r + 1) * DRAFT)
            pick = jnp.concatenate(
                [one_hot(buf_cols == slots_ref[rows, t : t + 1]) for t in range(TOPK)], axis=0
            )
            cos = jnp.concatenate([cos_ref[rows]] * TOPK, axis=0)
            sin = jnp.concatenate([sin_ref[rows]] * TOPK, axis=0)
            for h in range(part * 4, part * 4 + 4, 2):
                raw = jnp.dot(pick, back_ref[:, h * HD : (h + 2) * HD], preferred_element_type=F32)
                for one in range(2):
                    head = raw[:, one * HD : (one + 1) * HD]
                    mine_ref[r, :, head_rows(h + one)] = rotate_head(head, cos, sin).astype(BF16)
            mine = mine_ref.at[r, :, cols]
            ring.send_own(r, mine)
            keep = pltpu.make_async_copy(mine, request_view(ring.own, r), load_sem.at[2 + 2 * part + r])
            keep.start()
            keeps.append(keep)

    trip = RoundTrip(
        (there_send, there_recv, back_send, back_recv), (routed_ref, arrived_ref, result_ref, back_ref),
        1, 2, prepare, project, turn,
    )
    trip.send(0, ready)
    meanwhile()
    trip.run()
    to_scalars.wait()

    def drain():
        trip.drain()
        for piece in pieces:
            piece.wait_send()

    return rings, keeps, drain


def head_rows(h):
    return slice(h * HD, (h + 1) * HD)


def value_cols(h):
    return slice(HEADW + h * HD, HEADW + (h + 1) * HD)


def head_rows(h):
    return slice(h * HD, (h + 1) * HD)


def value_cols(h):
    return slice(HEADW + h * HD, HEADW + (h + 1) * HD)


def block_attention(blocks):
    scores = [
        lax.dot_general(keys, queries, (((1,), (1,)), ((), ())), preferred_element_type=F32)
        for keys, _, queries, _ in blocks
    ]
    scores = [jnp.where(block[3], one, NEGATIVE_FILL) for one, block in zip(scores, blocks)]
    tops = [jnp.max(one, axis=0, keepdims=True) for one in scores]
    weights = [jnp.exp2((one - top) * EXP_SCALE) for one, top in zip(scores, tops)]
    totals = [jnp.sum(one, axis=0, keepdims=True) for one in weights]
    accs = [
        lax.dot_general(block[1], one.astype(BF16), (((0,), (0,)), ((), ())), preferred_element_type=F32)
        for one, block in zip(weights, blocks)
    ]
    return tops, totals, accs


def shares_of(lses):
    top = lses[0]
    for lse in lses[1:]:
        top = jnp.maximum(top, lse)
    raised = [jnp.exp(lse - top) for lse in lses]
    total = raised[0]
    for one in raised[1:]:
        total = total + one
    return [one / total for one in raised], top + jnp.log(total)


def merge_parts(parts, store):
    shares, lse = shares_of([part[1] for part in parts])
    for h in range(HALFH):
        rows = head_rows(h)
        merged = None
        for (values_of, _), share in zip(parts, shares):
            values = values_of(rows).astype(F32) * share[h : h + 1]
            merged = values if merged is None else merged + values
        store(rows, merged.astype(BF16))
    return lse


def home_stage(
    table_ref, kv_ref, reach_ref, slot_rows_ref, slots_ref, gates_ref, own_query, query_bufs, cache_bufs,
    cache_hbm, own_hbm, attn_ref,
    held_buf, held_lse, max_ref, sum_ref, acc_ref,
    out_sib, out_sib_lse, sib_buf, sib_lse, send_buf, send_lse, recv_buf, recv_lse, tree_buf, mixed_buf,
    halves_ref, placed_ref, arrived_ref, result_ref, back_ref,
    load_sem, sib_send, sib_recv, ring_send, ring_recv, there_send, there_recv, back_send, back_recv,
    swap_send, swap_recv, first_stage,
):
    place = lax.axis_index("exp")
    parity = place % 2
    partner = place + 1 - 2 * parity
    core, chip, chip_after, chip_before, chip_across = req_places()
    sibling = chip * 2 + 1 - core
    after, before = chip_after * 2 + core, chip_before * 2 + core

    load = pltpu.make_async_copy(own_hbm, halves_ref.at[parity], load_sem.at[0])
    page_loads = [[], []]
    for half in range(2):
        for quarter in range(4):
            pages = pl.ds(quarter * SLOTS // 4, SLOTS // 4)
            for n, start in enumerate((0, HEADW)):
                page_loads[half].append(
                    pltpu.make_async_copy(
                        cache_hbm.at[pages, :, pl.ds(start + half * HALFW, HALFW)],
                        cache_bufs[half].at[pages, :, pl.ds(n * HALFW, HALFW)],
                        load_sem.at[1 + half * 8 + quarter * 2 + n],
                    )
                )
    rings, keeps, first_drain = first_stage()
    load.start()
    for one in page_loads[0] + page_loads[1]:
        one.start()
    max_ref[...] = jnp.full_like(max_ref, NEGATIVE_FILL)
    sum_ref[...] = jnp.zeros_like(sum_ref)
    acc_ref[...] = jnp.zeros_like(acc_ref)

    chunk = own_hbm.shape[0] // (2 * CHUNKS)

    def chunk_of(which, n):
        return pl.ds(pl.multiple_of((which * CHUNKS + n) * chunk, 8), chunk)

    swaps = []
    for n in range(CHUNKS):
        rows = chunk_of(core, n)
        one = send_to(own_hbm.at[rows], halves_ref.at[parity, rows], swap_send.at[n], swap_recv.at[n], "exp", partner)
        one.start()
        swaps.append(one)

    def hand_on(n):
        place_here = halves_ref.at[1 - parity, chunk_of(core, n)]
        send_to(place_here, place_here, swap_send.at[n], swap_recv.at[n], "exp", partner).wait_recv()
        slot = CHUNKS + n
        one = send_to(place_here, place_here, swap_send.at[slot], swap_recv.at[slot], "req", sibling)
        one.start()
        swaps.append(one)

    def await_handed(n):
        place_here = halves_ref.at[1 - parity, chunk_of(1 - core, n)]
        slot = CHUNKS + n
        send_to(place_here, place_here, swap_send.at[slot], swap_recv.at[slot], "req", sibling).wait_recv()

    tree_lses = [[None, None], [None, None]]

    def attend_tree():
        for r in range(REQ_X):
            tokens = slice(r * DRAFT, (r + 1) * DRAFT)
            valid = reach_ref[r] > 0.5
            tops, totals, accs = block_attention([
                (kv_ref[tokens, head_rows(h)], kv_ref[tokens, value_cols(h)], own_query[r, :, head_rows(h)], valid)
                for h in range(KVH)
            ])
            for half in range(2):
                mine = slice(half * HALFH, (half + 1) * HALFH)
                top, total = jnp.concatenate(tops[mine], axis=0), jnp.concatenate(totals[mine], axis=0)
                inverse = 1.0 / total
                for h, acc in enumerate(accs[mine]):
                    tree_buf[half, r, head_rows(h)] = (acc * inverse[h : h + 1]).astype(BF16)
                tree_lses[half][r] = top * SCALE + jnp.log(total)

    def index_at(row, column):
        return jnp.clip(table_ref[row, column], 0, SLOTS - 1)

    def attend(half, begin, end):
        def pair(p, carry):
            slots = [2 * p + n for n in range(2)]
            blocks = []
            for i in slots:
                at, request = index_at(i, 0), index_at(i, 1)
                valid = iota((PAGE, QROWS), 0) < table_ref[i, 2]
                for h in range(HALFH):
                    blocks.append((
                        cache_bufs[half][at, :, head_rows(h)], cache_bufs[half][at, :, head_rows(HALFH + h)],
                        query_bufs[half][request, :, head_rows(h)], valid,
                    ))
            tops, totals, accs = block_attention(blocks)
            for n, i in enumerate(slots):
                mine = slice(n * HALFH, (n + 1) * HALFH)
                page_max, page_sum = jnp.concatenate(tops[mine], axis=0), jnp.concatenate(totals[mine], axis=0)
                earlier = jnp.where(i == 0, -1, table_ref[jnp.maximum(i - 1, 0), 1])
                same = jnp.full(page_max.shape, earlier, jnp.int32) == table_ref[i, 1]
                old_max = jnp.where(same, max_ref[...], NEGATIVE_FILL)
                new_max = jnp.maximum(old_max, page_max)
                old_scale = jnp.exp2((old_max - new_max) * EXP_SCALE)
                page_scale = jnp.exp2((page_max - new_max) * EXP_SCALE)
                total = sum_ref[...] * old_scale + page_sum * page_scale
                max_ref[...] = new_max
                sum_ref[...] = total
                inverse = 1.0 / total
                held_lse[half, i] = new_max * SCALE + jnp.log(total)
                for h, acc in enumerate(accs[mine]):
                    rows = head_rows(h)
                    merged = acc_ref[rows] * old_scale[h : h + 1] + acc * page_scale[h : h + 1]
                    acc_ref[rows] = merged
                    held_buf[half, i, rows] = (merged * inverse[h : h + 1]).astype(BF16)
            return carry

        lax.fori_loop(begin, end, pair, 0)

    def lse_of(half, request):
        lse = held_lse[half, index_at(request, 3)]
        return jnp.where(jnp.full(lse.shape, table_ref[request, 4], jnp.int32) > 0, lse, NEGATIVE_FILL)

    def held_of(half, request):
        return (lambda rows: held_buf[half, index_at(request, 3), rows]), lse_of(half, request)

    owners = [chip_across, chip_after, chip_before, chip]

    def swap_cores(half):
        copies = []
        for k, owner in enumerate(owners):
            for r in range(REQ_X):
                request = (owner * 2 + 1 - core) * REQ_X + r
                out_sib[half, k, r] = held_buf[half, index_at(request, 3)]
                out_sib_lse[half, k, r] = lse_of(half, request)
            slot = half * 8 + 2 * k
            pair = [
                send_to(src.at[half, k], dst.at[half, k], sib_send.at[slot + n], sib_recv.at[slot + n], "req", sibling)
                for n, (src, dst) in enumerate(((out_sib_lse, sib_lse), (out_sib, sib_buf)))
            ]
            for one in pair:
                one.start()
            copies.append(pair)
        return copies

    def chip_parts(half, k, r):
        return [
            held_of(half, (owners[k] * 2 + core) * REQ_X + r),
            ((lambda rows: sib_buf[half, k, r, rows]), sib_lse[half, k, r]),
        ]

    def came(half, slot):
        return (lambda rows: recv_buf[half, slot, rows]), recv_lse[half, slot]

    def relay(half, slot, parts, peer):
        def store(rows, values):
            send_buf[half, slot, rows] = values

        send_lse[half, slot] = merge_parts(parts, store)
        sem = half * 12 + 2 * slot
        pair = [
            send_to(src.at[half, slot], dst.at[half, slot], ring_send.at[sem + n], ring_recv.at[sem + n], "req", peer)
            for n, (src, dst) in enumerate(((send_lse, recv_lse), (send_buf, recv_buf)))
        ]
        for one in pair:
            one.start()
        return pair

    def arrive(copies):
        for one in copies:
            one.wait_recv()

    sib, ring = [None, None], [{}, {}]

    def ring_start(half):
        arrive(sib[half][0])
        ring[half][0] = relay(half, 0, chip_parts(half, 0, 0), after)
        ring[half][1] = relay(half, 1, chip_parts(half, 0, 1), before)
        arrive(sib[half][1])
        ring[half][2] = relay(half, 2, chip_parts(half, 1, 1), after)
        arrive(sib[half][2])
        ring[half][3] = relay(half, 3, chip_parts(half, 2, 0), before)

    def ring_relay(half):
        arrive(ring[half][0])
        ring[half][4] = relay(half, 4, chip_parts(half, 1, 0) + [came(half, 0)], after)
        arrive(ring[half][1])
        ring[half][5] = relay(half, 5, chip_parts(half, 2, 1) + [came(half, 1)], before)

    def ring_end(half):
        arrive(sib[half][3])
        for slot in (2, 3, 4, 5):
            arrive(ring[half][slot])
        for r in range(REQ_X):
            parts = chip_parts(half, 3, r) + [came(half, s) for s in ((4, 3), (2, 5))[r]]
            parts.append(((lambda rows: tree_buf[half, r, rows]), tree_lses[half][r]))

            def store(rows, values):
                mixed_buf[half, r, rows] = values

            merge_parts(parts, store)

    def prepare(first, rows, part):
        slot = group_slots(first, QROWS)
        total = None
        for r in range(REQ_X):
            spread = one_hot(slot == slot_rows_ref[r : r + 1, :])
            one = lax.dot_general(spread, mixed_buf[part, r], (((1,), (1,)), ((), ())), preferred_element_type=F32)
            total = one if total is None else total + one
        placed_ref[rows, part * HALFW : (part + 1) * HALFW] = total.astype(BF16)

    def project(rows, part):
        for n in range(D // PARTS // 512):
            cols = slice(part * D // PARTS + n * 512, part * D // PARTS + (n + 1) * 512)
            total = None
            for half in range(2):
                one = jnp.dot(
                    arrived_ref[rows, half * HALFW : (half + 1) * HALFW], halves_ref[half, :, cols],
                    preferred_element_type=F32,
                )
                total = one if total is None else total + one
            result_ref[rows, cols] = total.astype(BF16)

    buf_cols = iota((ROWS, BUF), 1)

    def combine(part):
        for n in range(D // PARTS // 512):
            cols = slice(part * D // PARTS + n * 512, part * D // PARTS + (n + 1) * 512)
            total = None
            for t in range(TOPK):
                pick = one_hot(buf_cols == slots_ref[:, t : t + 1])
                one = jnp.dot(pick, back_ref[:, cols], preferred_element_type=F32) * gates_ref[:, t : t + 1]
                total = one if total is None else total + one
            attn_ref[:, cols] = total.astype(BF16)

    trip = RoundTrip(
        (there_send, there_recv, back_send, back_recv), (placed_ref, arrived_ref, result_ref, back_ref),
        2, PARTS, prepare, project, combine,
    )
    rings[0].relay()
    rings[0].relay_across()
    attend_tree()
    for one in page_loads[0] + keeps[:REQ_X]:
        one.wait()
    rings[0].finish()
    attend(0, 0, SLOTS // 4)
    rings[1].relay()
    attend(0, SLOTS // 4, SLOTS // 2)
    rings[1].relay_across()
    sib[0] = swap_cores(0)
    for one in page_loads[1] + keeps[REQ_X:]:
        one.wait()
    rings[1].finish()
    attend(1, 0, SLOTS // 4)
    ring_start(0)
    attend(1, SLOTS // 4, SLOTS // 2)
    sib[1] = swap_cores(1)
    ring_relay(0)
    ring_start(1)
    ring_end(0)
    trip.send(0)
    for n in range(CHUNKS):
        hand_on(n)
    ring_relay(1)
    ring_end(1)
    trip.send(1)
    load.wait()
    for n in range(CHUNKS):
        await_handed(n)
    trip.run()
    trip.drain()
    first_drain()
    for copies in sib[0] + sib[1] + list(ring[0].values()) + list(ring[1].values()) + [swaps]:
        for one in copies:
            one.wait_send()


def layer_kernel(*refs):
    refs = list(refs)

    def take(n):
        taken = refs[:n]
        del refs[:n]
        return taken

    small = take(9)
    query_hbm, kv_hbm, cache_hbm, out_hbm = take(4)
    cache_ref, attn_ref = take(2)
    query_bufs, cache_bufs = take(2), take(2)
    kv_ref, reach_ref, gates_ref, slots_ref, slot_rows_ref, table_wide, table_ref, mine_ref = take(8)
    first_buffers, first_sems = take(10), take(11)
    second = take(31)

    place = lax.axis_index("exp")
    core, chip, after, before, _ = req_places()
    barrier = pltpu.get_barrier_semaphore()
    for peer in (chip * 2 + 1 - core, after * 2 + core, before * 2 + core):
        pl.semaphore_signal(barrier, inc=1, device_id={"req": peer}, device_id_type=MESH)
    for peer in [place + 1 - 2 * (place % 2)] + [expert_peer(k) for k in range(1, EXPERTS)]:
        pl.semaphore_signal(barrier, inc=1, device_id={"exp": peer}, device_id_type=MESH)

    def enter():
        pl.semaphore_wait(barrier, 3 + EXPERTS)

    def first_stage():
        return query_stage(
            *small, query_hbm, kv_hbm, query_bufs, cache_ref,
            kv_ref, reach_ref, gates_ref, slots_ref, slot_rows_ref, table_wide, table_ref, mine_ref,
            *first_buffers, *first_sems, enter,
        )

    home_stage(
        table_ref, kv_ref, reach_ref, slot_rows_ref, slots_ref, gates_ref, mine_ref, query_bufs, cache_bufs,
        cache_hbm, out_hbm, attn_ref, *second, first_stage,
    )


def layer(hidden, choice, router, counts, tails, perm, parents, leaf, freq, w_query, w_kv, cache, w_out):
    places, holders = lax.axis_size("exp"), lax.axis_size("req")
    chips, requests = holders // 2, counts.shape[1]
    part, rows = (HALFW, QROWS), (HALFH, QROWS)
    vmem, hbm = pl.BlockSpec(memory_space=VMEM), pl.BlockSpec(memory_space=pl.ANY)
    return pl.pallas_call(
        layer_kernel,
        out_shape=(
            jax.ShapeDtypeStruct((ROWS, 2 * HEADW), BF16),
            jax.ShapeDtypeStruct((ROWS, D), BF16),
        ),
        in_specs=[vmem] * 9 + [hbm] * 4,
        out_specs=(vmem, vmem),
        scratch_shapes=[
            VMEM((requests, QROWS, HALFW), BF16),
            VMEM((requests, QROWS, HALFW), BF16),
            VMEM((SLOTS, PAGE, 2 * HALFW), BF16),
            VMEM((SLOTS, PAGE, 2 * HALFW), BF16),
            VMEM((ROWS, 2 * HEADW), BF16),
            VMEM((REQ_X, DRAFT, QROWS), F32),
            VMEM((ROWS, TOPK), F32),
            VMEM((ROWS, TOPK), jnp.int32),
            VMEM((REQ_X, QROWS), jnp.int32),
            VMEM((SLOTS, HD), jnp.int32),
            pltpu.SMEM((SLOTS, HD), jnp.int32),
            VMEM((REQ_X, QROWS, HEADW), BF16),
            VMEM((ROWS, D), BF16),
            VMEM((BUF, D), BF16),
            VMEM((BUF, D), BF16),
            VMEM((BUF, HEADW), BF16),
            VMEM((BUF, HEADW), BF16),
            VMEM((2,) + w_query.shape, BF16),
            VMEM(w_kv.shape, BF16),
            VMEM((ROWS, HD), F32),
            VMEM((ROWS, HD), F32),
            VMEM((REQ_X, DRAFT, HD), F32),
            DMA((7,)),
        ]
        + [DMA((places,))] * 2
        + [DMA((2 * places,))] * 2
        + [DMA((2,))] * 2
        + [DMA((Gather.SLOTS,))] * 2
        + [DMA((2, Gather.SLOTS))] * 2
        + [
            VMEM((2, SLOTS) + part, BF16),
            VMEM((2, SLOTS) + rows, F32),
            VMEM(rows, F32),
            VMEM(rows, F32),
            VMEM(part, F32),
            VMEM((2, chips, REQ_X) + part, BF16),
            VMEM((2, chips, REQ_X) + rows, F32),
            VMEM((2, chips, REQ_X) + part, BF16),
            VMEM((2, chips, REQ_X) + rows, F32),
            VMEM((2, 6) + part, BF16),
            VMEM((2, 6) + rows, F32),
            VMEM((2, 6) + part, BF16),
            VMEM((2, 6) + rows, F32),
            VMEM((2, REQ_X) + part, BF16),
            VMEM((2, REQ_X) + part, BF16),
            VMEM((2,) + w_out.shape, BF16),
            VMEM((BUF, HEADW), BF16),
            VMEM((BUF, HEADW), BF16),
            VMEM((BUF, D), BF16),
            VMEM((BUF, D), BF16),
            DMA((17,)),
            DMA((4 * chips,)),
            DMA((4 * chips,)),
            DMA((24,)),
            DMA((24,)),
            DMA((2 * places,)),
            DMA((2 * places,)),
            DMA((PARTS * places,)),
            DMA((PARTS * places,)),
            DMA((2 * CHUNKS,)),
            DMA((2 * CHUNKS,)),
        ],
        compiler_params=pltpu.CompilerParams(
            collective_id=0, has_side_effects=True, vmem_limit_bytes=67_000_000
        ),
        name="layer",
    )(hidden, choice, router, counts, tails, perm, parents, leaf, freq, w_query, w_kv, cache, w_out)


def body(
    hidden_in,
    router_choice,
    w_router,
    w_kv,
    w_query,
    w_out,
    kv_cache,
    page_count,
    tail_len,
    page_perm,
    parents,
    accepted_leaf,
):
    half = HD // 2
    freq = np.tile(10000.0 ** (-np.arange(half) / half), 2).astype(np.float32)[None, :]
    cache_rows, attn_out = layer(
        hidden_in.reshape(ROWS, D),
        jnp.swapaxes(router_choice[0], 1, 2),
        w_router.T,
        page_count,
        tail_len,
        page_perm,
        parents[0],
        accepted_leaf,
        jnp.asarray(freq),
        w_query[0],
        w_kv,
        kv_cache[0],
        w_out[0],
    )
    return (attn_out.reshape(1, REQ_X, DRAFT, D), cache_rows.reshape(1, REQ_X, DRAFT, 2 * HEADW))


def solution(mesh):
    placed = (
        P("exp", "req", None, None),
        P("exp", "req", None, None),
        P(),
        P(),
        P("exp", None, None),
        P("exp", None, None),
        P("exp", "req", None, None),
        P("exp", None),
        P("exp", None),
        P("exp", None),
        P("exp", "req", None),
        P("exp", "req"),
    )
    return jax.shard_map(
        body,
        mesh=mesh,
        in_specs=placed,
        out_specs=(P("exp", "req", None, None), P("exp", "req", None, None)),
        check_vma=False,
    )
```
